32 devices in a mesh: gx: 2 (over x), gy: 4 (over z), gz: 4 (over y, core).
Axes of the slice: x: 2, y: 2, z: 4, core: 2. Of those that a mesh axis runs over, the one named last changes fastest.
Arguments:
- order_parameter: float32 [8, 512, 512], P('gx', 'gy', 'gz'), may hold values from -1 to 1
- dissolved_species: float32 [8, 512, 512], P('gx', 'gy', 'gz'), may hold values from -0.8 to 0.2
- broad_undercool: float32 [128, 128, 2], P('gy', 'gz'), may hold values from -2.4 to 2.4
Outputs:
- phase_out: float32 [8, 512, 512], P('gx', 'gy', 'gz')
- solute_out: float32 [8, 512, 512], P('gx', 'gy', 'gz')
- temperature_out: float32 [128, 128, 2], P('gy', 'gz')
The draws below stay inside these ranges and needn't reach their ends.
All inputs are finite; a program needn't handle non-finite values.
Results may differ from the reference program's by a relative error of at most 0.0001.
Values sent between devices are 32-bit elements; how exact they have to be, the bound alone decides.
No kernel may reach another device: no remote copies, remote signals or barrier semaphores. Data moves between devices by JAX's collectives and lax.ppermute only.
A program may use at most 64 MiB of HBM per device.

```python
import jax
import jax.numpy as jnp

FACTOR = 4
SUBSTEPS = 4
NX = 8
NY = 512
NZ = 512
BROAD_COUNT_ONE = 2
BROAD_COUNT_TWO = 128
BROAD_COUNT_THREE = 128


def shard_levels(key, dims, pieces, smallest, largest):
    level, own = 1.0, jax.random.fold_in(key, 6)
    for axis_at, parts in pieces:
        steps = jnp.exp(jax.random.uniform(jax.random.fold_in(own, axis_at), (parts,), jnp.float32, smallest / len(pieces), largest / len(pieces)))
        level = level * jnp.repeat(steps, dims[axis_at] // parts).reshape([-1 if axis == axis_at else 1 for axis in range(len(dims))])
    return level


def noise(stream_key, extent, width, bound, cuts=(), dtype=jnp.bfloat16):
    entries = width * jax.random.normal(stream_key, extent, jnp.float32)
    if cuts:
        entries = entries * shard_levels(stream_key, extent, cuts, -0.22, 0.18)
    return jnp.clip(entries, -bound, bound).astype(dtype)


def setup_inputs(seed: int = 0) -> dict:
    keys = jax.random.split(jax.random.key(seed), 4)
    order_parameter = jnp.clip(jax.random.uniform(keys[0], (NX, NY, NZ), jnp.float32, -1.0, 1.0) * shard_levels(keys[0], (NX, NY, NZ), ((0, 2), (1, 4), (2, 4)), -0.4, 0.0), -1.0, 1.0)
    dissolved_species = jnp.clip(-0.8 + 1 * jax.random.uniform(keys[1], (NX, NY, NZ), jnp.float32) ** shard_levels(keys[1], (NX, NY, NZ), ((0, 2), (1, 4), (2, 4)), -0.2, 0.2), -0.8, 0.2)
    broad_undercool = noise(keys[2], (BROAD_COUNT_TWO, BROAD_COUNT_THREE, BROAD_COUNT_ONE), 0.4, 2.4, ((0, 4), (1, 4)), jnp.float32)
    return {"order_parameter": order_parameter, "dissolved_species": dissolved_species, "broad_undercool": broad_undercool}


TIME_INCREMENT = 0.1
COUPLING = 3.0
PARTITION = 0.3
DIFFUSION = 1.0
THERMAL_SPREAD = 1.2
FREEZING_WARMTH = 2.0


def second_derivative_sum(field):
    total = -6.0 * field
    for axis_id in range(3):
        total = total + jnp.roll(field, 1, axis_id) + jnp.roll(field, -1, axis_id)
    return total


def faces_flux(values, mobility):
    total = jnp.zeros_like(values)
    for axis_id in range(3):
        upper_v = jnp.roll(values, -1, axis_id)
        lower_v = jnp.roll(values, 1, axis_id)
        upper_m = jnp.roll(mobility, -1, axis_id)
        lower_m = jnp.roll(mobility, 1, axis_id)
        total = total + 0.5 * (upper_m + mobility) * (upper_v - values) - 0.5 * (mobility + lower_m) * (values - lower_v)
    return total


def reference(order_parameter, dissolved_species, broad_undercool):
    for substep in range(SUBSTEPS):
        vertical_pile = jnp.transpose(broad_undercool, (2, 0, 1))
        fine_temp = jnp.repeat(jnp.repeat(jnp.repeat(vertical_pile, FACTOR, 0), FACTOR, 1), FACTOR, 2)
        square = 1.0 - order_parameter * order_parameter
        driving = second_derivative_sum(order_parameter) + order_parameter - order_parameter * order_parameter * order_parameter - COUPLING * square * square * (dissolved_species + fine_temp)
        new_phase = jnp.clip(order_parameter + TIME_INCREMENT * driving, -1.0, 1.0)
        change = new_phase - order_parameter
        mobility = 0.5 * (1.0 - new_phase)
        numer = TIME_INCREMENT * DIFFUSION * faces_flux(dissolved_species, mobility) + 0.5 * (1.0 + (1.0 - PARTITION) * dissolved_species) * change
        new_solute = dissolved_species + numer / (0.5 * (1.0 + PARTITION - (1.0 - PARTITION) * new_phase))
        blocks = (0.5 * change).reshape(BROAD_COUNT_ONE, FACTOR, BROAD_COUNT_TWO, FACTOR, BROAD_COUNT_THREE, FACTOR)
        freezing_warmth_source = jnp.transpose(jnp.mean(blocks, axis=(1, 3, 5)), (1, 2, 0))
        broad_undercool = broad_undercool + TIME_INCREMENT * THERMAL_SPREAD * second_derivative_sum(broad_undercool) + FREEZING_WARMTH * freezing_warmth_source
        order_parameter = new_phase
        dissolved_species = new_solute
    return order_parameter, dissolved_species, broad_undercool
```

```python
import functools

import jax
import jax.numpy as jnp
from jax import lax
from jax.experimental import pallas as pl
from jax.experimental.pallas import tpu as pltpu
from jax.sharding import PartitionSpec as P

FACTOR = 4
SUBSTEPS = 4

TIME_INCREMENT = 0.1
COUPLING = 3.0
PARTITION = 0.3
DIFFUSION = 1.0
THERMAL_SPREAD = 1.2
FREEZING_WARMTH = 2.0

LANES = 128
ROWS = 8
HALO = FACTOR * SUBSTEPS
SLOT = 2 * HALO
PER_TILE = LANES // SLOT


def padded_2(cells, sides, width):
    for axis, dim in sides:
        count = lax.axis_size(axis)
        head = lax.slice_in_dim(cells, 0, width, axis=dim)
        tail = lax.slice_in_dim(cells, cells.shape[dim] - width, cells.shape[dim], axis=dim)
        cells = jnp.concatenate(
            [
                lax.ppermute(tail, axis, [(i, (i + 1) % count) for i in range(count)]),
                cells,
                lax.ppermute(head, axis, [((i + 1) % count, i) for i in range(count)]),
            ],
            axis=dim,
        )
    return cells


def laplace_padded(padded):
    center = padded[1:-1, 1:-1, 1:-1]
    total = padded[2:, 1:-1, 1:-1] + padded[:-2, 1:-1, 1:-1]
    total = total + padded[1:-1, 2:, 1:-1] + padded[1:-1, :-2, 1:-1]
    total = total + padded[1:-1, 1:-1, 2:] + padded[1:-1, 1:-1, :-2]
    return total - 6.0 * center


def flux_padded(values, mobility):
    center_v = values[1:-1, 1:-1, 1:-1]
    center_m = mobility[1:-1, 1:-1, 1:-1]
    total = jnp.zeros_like(center_v)
    pairs = (
        (
            values[2:, 1:-1, 1:-1],
            values[:-2, 1:-1, 1:-1],
            mobility[2:, 1:-1, 1:-1],
            mobility[:-2, 1:-1, 1:-1],
        ),
        (
            values[1:-1, 2:, 1:-1],
            values[1:-1, :-2, 1:-1],
            mobility[1:-1, 2:, 1:-1],
            mobility[1:-1, :-2, 1:-1],
        ),
        (
            values[1:-1, 1:-1, 2:],
            values[1:-1, 1:-1, :-2],
            mobility[1:-1, 1:-1, 2:],
            mobility[1:-1, 1:-1, :-2],
        ),
    )
    for upper_v, lower_v, upper_m, lower_m in pairs:
        total = (
            total
            + 0.5 * (upper_m + center_m) * (upper_v - center_v)
            - 0.5 * (center_m + lower_m) * (center_v - lower_v)
        )
    return total


def phase_update(phase_pad, centre_phase, centre_solute, centre_temp):
    square = 1.0 - centre_phase * centre_phase
    driving = (
        laplace_padded(phase_pad)
        + centre_phase
        - centre_phase * centre_phase * centre_phase
        - COUPLING * square * square * (centre_solute + centre_temp)
    )
    return jnp.clip(centre_phase + TIME_INCREMENT * driving, -1.0, 1.0)


def stepwise(order_parameter, dissolved_species, broad_undercool):
    size_x, size_y, size_z = order_parameter.shape
    coarse_x = size_x // FACTOR
    coarse_y = size_y // FACTOR
    coarse_z = size_z // FACTOR
    start_x = lax.axis_index("gx") * coarse_x
    own_block = lax.dynamic_slice_in_dim(broad_undercool, start_x, coarse_x, 2)
    for substep in range(SUBSTEPS):
        planes = own_block
        local_col = jnp.transpose(planes, (2, 0, 1))
        fine_temp = jnp.repeat(jnp.repeat(jnp.repeat(local_col, FACTOR, 0), FACTOR, 1), FACTOR, 2)
        stacked = jnp.stack([order_parameter, dissolved_species])
        padded = padded_2(stacked, (("gx", 1), ("gy", 2), ("gz", 3)), 1)
        solute_pad = padded[1]
        new_phase = phase_update(padded[0], order_parameter, dissolved_species, fine_temp)
        new_pad = padded_2(new_phase, (("gx", 0), ("gy", 1), ("gz", 2)), 1)
        mobility = 0.5 * (1.0 - new_pad)
        change = new_phase - order_parameter
        numer = (
            TIME_INCREMENT * DIFFUSION * flux_padded(solute_pad, mobility)
            + 0.5 * (1.0 + (1.0 - PARTITION) * dissolved_species) * change
        )
        new_solute = dissolved_species + numer / (
            0.5 * (1.0 + PARTITION - (1.0 - PARTITION) * new_phase)
        )
        blocks = (0.5 * change).reshape(coarse_x, FACTOR, coarse_y, FACTOR, coarse_z, FACTOR)
        freezing_warmth_source = jnp.transpose(jnp.mean(blocks, axis=(1, 3, 5)), (1, 2, 0))
        block_pad = padded_2(own_block, (("gx", 2), ("gy", 0), ("gz", 1)), 1)
        own_block = (
            own_block
            + TIME_INCREMENT * THERMAL_SPREAD * laplace_padded(block_pad)
            + FREEZING_WARMTH * freezing_warmth_source
        )
        order_parameter = new_phase
        dissolved_species = new_solute
    vertical_pile = lax.all_gather(own_block, "gx", axis=2, tiled=True)
    return (order_parameter, dissolved_species, vertical_pile)


def lane_index(shape):
    return lax.broadcasted_iota(jnp.int32, shape, 1)


def turn(tile, shift):
    shift = shift % LANES
    return tile if shift == 0 else pltpu.roll(tile, shift, 1)


def choose(pairs, shape, width):
    group = lane_index(shape) // width
    out = pairs[0][1]
    for index, tile in pairs[1:]:
        out = jnp.where(group == index, tile, out)
    return out


def spread_matrix(rows, cols, by_row):
    i = lax.broadcasted_iota(jnp.int32, (rows, cols), 0)
    j = lax.broadcasted_iota(jnp.int32, (rows, cols), 1)
    same = (i // FACTOR == j) if by_row else (i == j // FACTOR)
    return same.astype(jnp.float32)


def pick_matrix(rows, cols, by_row):
    i = lax.broadcasted_iota(jnp.int32, (rows, cols), 0)
    j = lax.broadcasted_iota(jnp.int32, (rows, cols), 1)
    same = (j == i * FACTOR) if by_row else (i == j * FACTOR)
    return same.astype(jnp.float32)


def exact_dot(a, b):
    return jnp.dot(a, b, precision=lax.Precision.HIGHEST, preferred_element_type=jnp.float32)


def pack_kernel(me_ref, p_ref, u_ref, t_ref, ylo, yhi, zlo, zhi, cll, clh, chl, chh, tf_ref):
    size_x, size_y, _ = p_ref.shape
    first = me_ref[0] == 0
    wide = spread_matrix(size_y, t_ref.shape[0], True)
    long = spread_matrix(t_ref.shape[2], LANES, False)
    layers = [exact_dot(exact_dot(wide, t_ref[:, g, :]), long) for g in range(2)]
    for g in range(2):
        tf_ref[g] = jnp.where(first, layers[g], layers[1 - g])
    sources = [p_ref.at[i] for i in range(size_x)] + [u_ref.at[i] for i in range(size_x)] + [tf_ref.at[g] for g in range(2)]
    shape = (HALO, LANES)
    parts = size_y // HALO
    per = LANES // HALO
    low, high = pl.ds(0, HALO), pl.ds(size_y - HALO, HALO)
    for i, src in enumerate(sources):
        ylo[i] = src[low, :]
        yhi[i] = src[high, :]
        rows = [src[pl.ds(HALO * g, HALO), :] for g in range(parts)]
        zlo[i] = choose([(g, turn(rows[g], HALO * g)) for g in range(parts)], shape, HALO)
        zhi[i] = choose([(g, turn(rows[g], HALO * g + HALO)) for g in range(parts)], shape, HALO)
    for tile in range(-(-len(sources) // per)):
        some = list(enumerate(sources))[tile * per : (tile + 1) * per]
        for rows, left, right in ((low, cll, clh), (high, chl, chh)):
            left[tile] = choose([(i % per, turn(s[rows, :], HALO * (i % per))) for i, s in some], shape, HALO)
            right[tile] = choose([(i % per, turn(s[rows, :], HALO * (i % per) + HALO)) for i, s in some], shape, HALO)


def ring_kernel(ylo, yhi, zlo, zhi, cll, clh, chl, chh, out):
    n = out.shape[0] // 9 * 2
    for k, src in enumerate((ylo, yhi, zlo, zhi)):
        out[pl.ds(k * n, n)] = src[pl.ds(0, n)]
    for k, src in enumerate((cll, clh, chl, chh)):
        out[4 * n + k] = src[0]


def step_kernel(
    me_ref, p_ref, u_ref, tf_ref, pp_ref, up_ref,
    ylo, yhi, zlo, zhi, cll, clh, chl, chh, ring,
    po_ref, uo_ref, to_ref,
    pc0, pc1, ph0, ph1, uc0, uc1, uh0, uh1, tc0, tc1, th0, th1, sc, sh,
):
    size_x, size_y, _ = p_ref.shape
    planes = 2 * size_x
    top = ROWS + HALO
    parts = size_y // HALO
    shape2 = (HALO, LANES)
    tile = (ROWS, LANES)
    lane = lane_index(tile)
    row = lax.broadcasted_iota(jnp.int32, tile, 0)
    n = planes

    before, inside, after = pl.ds(ROWS, HALO), pl.ds(top, size_y), pl.ds(top + size_y, HALO)

    def halo_tiles(pieces, slots):
        pairs = []
        for k in range(slots):
            left, at_left, right, at_right = pieces[k]
            pairs.append((2 * k, turn(right, SLOT * k - at_right)))
            pairs.append((2 * k + 1, turn(left, SLOT * k + HALO - at_left)))
        return choose(pairs, shape2, HALO)

    def place(core, side, group, own_rows, edge_low, edge_high, strip, corner):
        for k, (rows, lo, hi) in enumerate(zip(own_rows, edge_low, edge_high, strict=True)):
            core[group * len(own_rows) + k, before, :] = lo
            core[group * len(own_rows) + k, inside, :] = rows
            core[group * len(own_rows) + k, after, :] = hi
        side[group, before, :] = halo_tiles(corner(0), PER_TILE)
        side[group, after, :] = halo_tiles(corner(1), PER_TILE)
        for j in range(parts):
            pieces = [(l, HALO * j, r, HALO * j) for l, r in strip]
            side[group, pl.ds(top + HALO * j, HALO), :] = halo_tiles(pieces, PER_TILE)

    for field, (core, side, own, other) in enumerate(((pc0, ph0, p_ref, pp_ref), (uc0, uh0, u_ref, up_ref))):
        base = field * size_x
        own_corner = ((cll, clh), (chl, chh))
        place(
            core, side, 0,
            [own[k] for k in range(size_x)],
            [ylo[base + k] for k in range(size_x)],
            [yhi[base + k] for k in range(size_x)],
            [(zlo[base + k], zhi[base + k]) for k in range(size_x)],
            lambda e: [(own_corner[e][0][0], HALO * (base + k), own_corner[e][1][0], HALO * (base + k)) for k in range(size_x)],
        )
        place(
            core, side, 1,
            [other[k] for k in range(size_x)],
            [ring[base + k] for k in range(size_x)],
            [ring[n + base + k] for k in range(size_x)],
            [(ring[2 * n + base + k], ring[3 * n + base + k]) for k in range(size_x)],
            lambda e: [(ring[4 * n + 2 * e], HALO * (base + k), ring[4 * n + 2 * e + 1], HALO * (base + k)) for k in range(size_x)],
        )
    for g in range(2):
        place(
            tc0, th0, g,
            [tf_ref[g]],
            [ylo[n + g]],
            [yhi[n + g]],
            [(zlo[n + g], zhi[n + g])] * PER_TILE,
            lambda e: [(own_corner[e][0][1], HALO * g, own_corner[e][1][1], HALO * g)] * PER_TILE,
        )

    def up_z(cores, side, reach=1):
        slot = lambda k: k if len(cores) > 1 else 0
        out = [jnp.where(lane >= LANES - reach, turn(side, LANES - reach - SLOT * k), turn(c, -reach)) for k, c in enumerate(cores)]
        edge = turn(side, -reach)
        for k in range(PER_TILE):
            inside_slot = (lane >= SLOT * k + SLOT - reach) & (lane < SLOT * k + SLOT)
            edge = jnp.where(inside_slot, turn(cores[slot(k)], SLOT * k + SLOT - reach), edge)
        return out, edge

    def down_z(cores, side, reach=1):
        slot = lambda k: k if len(cores) > 1 else 0
        out = [jnp.where(lane < reach, turn(side, reach - SLOT * k - SLOT), turn(c, reach)) for k, c in enumerate(cores)]
        edge = turn(side, reach)
        for k in range(PER_TILE):
            inside_slot = (lane >= SLOT * k) & (lane < SLOT * k + reach)
            edge = jnp.where(inside_slot, turn(cores[slot(k)], SLOT * k + reach), edge)
        return out, edge

    def up_x_side(mine, others):
        return jnp.where(lane < LANES - SLOT, turn(mine, -SLOT), turn(others, -SLOT))

    def down_x_side(mine, others):
        return jnp.where(lane >= SLOT, turn(mine, SLOT), turn(others, SLOT))

    def pool(v):
        v = v + jnp.where(lane % 2 == 0, turn(v, -1), turn(v, 1))
        v = v + jnp.where(lane % 4 < 2, turn(v, -2), turn(v, 2))
        v = v + jnp.where(row % 2 == 0, pltpu.roll(v, ROWS - 1, 0), pltpu.roll(v, 1, 0))
        return v + jnp.where(row % 4 < 2, pltpu.roll(v, ROWS - 2, 0), pltpu.roll(v, 2, 0))

    def new_value(c, total, drive):
        c2 = c * c
        square = 1.0 - c2
        driving = total - c * (5.0 + c2) - (COUPLING * square * square) * drive
        return jnp.clip(c + TIME_INCREMENT * driving, -1.0, 1.0)

    def phase_pass(step, first_tile, last_tile):
        pa, pb = ((pc0, ph0), (pc1, ph1)) if step % 2 == 0 else ((pc1, ph1), (pc0, ph0))
        ua = (uc0, uh0) if step % 2 == 0 else (uc1, uh1)
        ta, tb = ((tc0, th0), (tc1, th1)) if step % 2 == 0 else ((tc1, th1), (tc0, th0))

        def body(r, _):
            at = pl.multiple_of(r * ROWS, ROWS)
            here, above, below = pl.ds(at, ROWS), pl.ds(at + 1, ROWS), pl.ds(at - 1, ROWS)
            far, near = pl.ds(at + FACTOR, ROWS), pl.ds(at - FACTOR, ROWS)
            ct = [ta[0][g, here, :] for g in range(2)]
            st = [ta[1][g, here, :] for g in range(2)]
            sides = [pa[1][g, here, :] for g in range(2)]
            for g in range(2):
                ks = range(g * size_x, (g + 1) * size_x)
                cores = [pa[0][k, here, :] for k in ks]
                if step == 0:
                    upc, ups = up_z(cores, sides[g])
                    dnc, dns = down_z(cores, sides[g])
                    totals = []
                    for i, k in enumerate(ks):
                        nxt = cores[i + 1] if i + 1 < size_x else pa[0][(k + 1) % planes, here, :]
                        prv = cores[i - 1] if i > 0 else pa[0][(k - 1) % planes, here, :]
                        totals.append(nxt + prv + upc[i] + dnc[i] + pa[0][k, above, :] + pa[0][k, below, :])
                    total_side = (
                        up_x_side(sides[g], sides[1 - g]) + down_x_side(sides[g], sides[1 - g])
                        + ups + dns + pa[1][g, above, :] + pa[1][g, below, :]
                    )
                else:
                    totals = [sc[k, here, :] for k in ks]
                    total_side = sh[g, here, :]
                heat = None
                for i, k in enumerate(ks):
                    new = new_value(cores[i], totals[i], ua[0][k, here, :] + ct[g])
                    pb[0][k, here, :] = new
                    change = new - cores[i]
                    heat = change if heat is None else heat + change
                new = new_value(sides[g], total_side, ua[1][g, here, :] + st[g])
                pb[1][g, here, :] = new
                heat_side = new - sides[g]
                width = SLOT
                while width < LANES:
                    heat_side = heat_side + turn(heat_side, width)
                    width *= 2
                upc, ups = up_z([ct[g]], st[g], FACTOR)
                dnc, dns = down_z([ct[g]], st[g], FACTOR)
                scale = FREEZING_WARMTH * 0.5 / FACTOR**3
                spread = TIME_INCREMENT * THERMAL_SPREAD
                for mine, other, up, down, ref_a, ref_b, source in (
                    (ct[g], ct[1 - g], upc[0], dnc[0], ta[0], tb[0], heat),
                    (st[g], st[1 - g], ups, dns, ta[1], tb[1], heat_side),
                ):
                    around = 2.0 * other + up + down + ref_a[g, far, :] + ref_a[g, near, :]
                    ref_b[g, here, :] = mine + spread * (around - 6.0 * mine) + scale * pool(source)

        lax.fori_loop(first_tile, last_tile, body, None)

    def solute_pass(step, first_tile, last_tile, last):
        pa, pb = ((pc0, ph0), (pc1, ph1)) if step % 2 == 0 else ((pc1, ph1), (pc0, ph0))
        ua, ub = ((uc0, uh0), (uc1, uh1)) if step % 2 == 0 else ((uc1, uh1), (uc0, uh0))

        def finish(u, p, p_old, flux):
            change = p - p_old
            numer = (0.25 * TIME_INCREMENT * DIFFUSION) * flux + (0.5 + 0.5 * (1.0 - PARTITION) * u) * change
            return u + numer / (0.5 * (1.0 + PARTITION) - 0.5 * (1.0 - PARTITION) * p)

        def cell(u, p, p_old, xs, ys, face, face_down, pz):
            near = [*xs, *ys]
            total_u = near[0][0] + near[1][0] + near[2][0] + near[3][0]
            total_p = near[0][1] + near[1][1] + near[2][1] + near[3][1]
            total_w = near[0][0] * near[0][1] + near[1][0] * near[1][1] + near[2][0] * near[2][1] + near[3][0] * near[3][1]
            flux = (2.0 - p) * (total_u - 4.0 * u) + u * total_p - total_w + (face - face_down)
            return finish(u, p, p_old, flux), total_p + pz

        def body(r, _):
            at = pl.multiple_of(r * ROWS, ROWS)
            here, above, below = pl.ds(at, ROWS), pl.ds(at + 1, ROWS), pl.ds(at - 1, ROWS)
            su = [ua[1][g, here, :] for g in range(2)]
            sp = [pb[1][g, here, :] for g in range(2)]
            for g in range(1 if last else 2):
                ks = range(g * size_x, (g + 1) * size_x)
                cu = [ua[0][k, here, :] for k in ks]
                cp = [pb[0][k, here, :] for k in ks]
                upu, upu_s = up_z(cu, su[g])
                upp, upp_s = up_z(cp, sp[g])
                face = [(2.0 - (a + b)) * (c - d) for a, b, c, d in zip(upp, cp, upu, cu, strict=True)]
                face_s = (2.0 - (upp_s + sp[g])) * (upu_s - su[g])
                dnf, dnf_s = down_z(face, face_s)
                if not last:
                    dnp, dnp_s = down_z(cp, sp[g])
                for i, k in enumerate(ks):
                    far, near = (k + 1) % planes, (k - 1) % planes
                    nxt = (cu[i + 1], cp[i + 1]) if i + 1 < size_x else (ua[0][far, here, :], pb[0][far, here, :])
                    prv = (cu[i - 1], cp[i - 1]) if i > 0 else (ua[0][near, here, :], pb[0][near, here, :])
                    ys = [(ua[0][k, w, :], pb[0][k, w, :]) for w in (above, below)]
                    pz = 0.0 if last else upp[i] + dnp[i]
                    new, total = cell(cu[i], cp[i], pa[0][k, here, :], (nxt, prv), ys, face[i], dnf[i], pz)
                    if last:
                        uo_ref[k, pl.ds(pl.multiple_of(at - top, ROWS), ROWS), :] = new
                    else:
                        ub[0][k, here, :] = new
                        sc[k, here, :] = total
                if not last:
                    xs = [(f(su[g], su[1 - g]), f(sp[g], sp[1 - g])) for f in (up_x_side, down_x_side)]
                    ys = [(ua[1][g, w, :], pb[1][g, w, :]) for w in (above, below)]
                    new, total = cell(su[g], sp[g], pa[1][g, here, :], xs, ys, face_s, dnf_s, upp_s + dnp_s)
                    ub[1][g, here, :] = new
                    sh[g, here, :] = total

        lax.fori_loop(first_tile, last_tile, body, None)

    tiles = (2 * top + size_y) // ROWS
    edge = top // ROWS
    for step in range(SUBSTEPS):
        last = step == SUBSTEPS - 1
        skip = 1 if step == 0 else 2
        phase_pass(step, skip, tiles - skip)
        solute_pass(step, edge if last else 2, tiles - (edge if last else 2), last)

    pf, tcf = (pc0, tc0) if SUBSTEPS % 2 == 0 else (pc1, tc1)
    for k in range(size_x):
        po_ref[k] = pf[k, inside, :]
    first = me_ref[0] == 0
    thin = pick_matrix(to_ref.shape[0], size_y, True)
    short = pick_matrix(LANES, to_ref.shape[2], False)
    layers = [exact_dot(exact_dot(thin, tcf[g, inside, :]), short) for g in range(2)]
    for g in range(2):
        to_ref[:, g, :] = jnp.where(first, layers[g], layers[1 - g])


def shifted(x, dy, dz):
    ny, nz = lax.axis_size("gy"), lax.axis_size("gz")
    if dz == 0:
        return lax.ppermute(x, "gy", [(i, (i + dy) % ny) for i in range(ny)])
    if dy == 0:
        return lax.ppermute(x, "gz", [(i, (i + dz) % nz) for i in range(nz)])
    pairs = [(i * nz + j, (i + dy) % ny * nz + (j + dz) % nz) for i in range(ny) for j in range(nz)]
    return lax.ppermute(x, ("gy", "gz"), pairs)


def swapped(x):
    return lax.ppermute(x, "gx", [(0, 1), (1, 0)])


def at_once(order_parameter, dissolved_species, broad_undercool):
    size_x, size_y, size_z = order_parameter.shape
    f32 = jnp.float32
    planes = 2 * size_x
    me = lax.axis_index("gx").astype(jnp.int32).reshape(1)
    coarse = jnp.transpose(broad_undercool, (0, 2, 1))
    smem = pl.BlockSpec(memory_space=pltpu.SMEM)
    vmem = pl.BlockSpec(memory_space=pltpu.VMEM)
    shape = jax.ShapeDtypeStruct

    partner_p = swapped(order_parameter)
    partner_u = swapped(dissolved_species)

    strip = shape((planes + 2, HALO, LANES), f32)
    corner = shape((-(-(planes + 2) * HALO // LANES), HALO, LANES), f32)
    packed = pl.pallas_call(
        pack_kernel,
        out_shape=[strip] * 4 + [corner] * 4 + [shape((2, size_y, size_z), f32)],
        in_specs=[smem, vmem, vmem, vmem],
        out_specs=[vmem] * 9,
        name="pack",
    )(me, order_parameter, dissolved_species, coarse)
    fine = packed[8]
    moves = ((-1, 0), (1, 0), (0, -1), (0, 1), (-1, -1), (-1, 1), (1, -1), (1, 1))
    yhi, ylo, zhi, zlo, chh, chl, clh, cll = [shifted(x, dy, dz) for x, (dy, dz) in zip(packed[:8], moves, strict=True)]
    around = (ylo, yhi, zlo, zhi, cll, clh, chl, chh)
    ring = pl.pallas_call(
        ring_kernel,
        out_shape=shape((4 * planes + 4, HALO, LANES), f32),
        in_specs=[vmem] * 8,
        out_specs=vmem,
        name="ring",
    )(*around)
    partner_ring = swapped(ring)

    rows = size_y + 2 * (HALO + ROWS)
    core, side = pltpu.VMEM((planes, rows, LANES), f32), pltpu.VMEM((2, rows, LANES), f32)
    new_p, new_u, new_t = pl.pallas_call(
        step_kernel,
        out_shape=[shape(order_parameter.shape, f32), shape(dissolved_species.shape, f32), shape(coarse.shape, f32)],
        in_specs=[smem] + [vmem] * 14,
        out_specs=[vmem] * 3,
        scratch_shapes=[core, core, side, side] * 2 + [side, side, side, side] + [core, side],
        name="steps",
    )(me, order_parameter, dissolved_species, fine, partner_p, partner_u, *around, partner_ring)
    return new_p, new_u, jnp.transpose(new_t, (0, 2, 1))


def per_device(order_parameter, dissolved_species, broad_undercool):
    size_x, size_y, size_z = order_parameter.shape
    whole_x = lax.axis_size("gx") == 2 and broad_undercool.shape[2] * FACTOR == 2 * size_x
    if whole_x and size_x == PER_TILE == FACTOR and size_y == size_z == LANES and PER_TILE * SLOT == LANES:
        return at_once(order_parameter, dissolved_species, broad_undercool)
    return stepwise(order_parameter, dissolved_species, broad_undercool)


def solution(mesh):
    return jax.shard_map(
        per_device,
        mesh=mesh,
        in_specs=(P("gx", "gy", "gz"), P("gx", "gy", "gz"), P("gy", "gz", None)),
        out_specs=(P("gx", "gy", "gz"), P("gx", "gy", "gz"), P("gy", "gz", None)),
        check_vma=False,
    )
```

```python
import functools

import jax
import jax.numpy as jnp
from jax import lax
from jax.experimental import pallas as pl
from jax.experimental.pallas import tpu as pltpu
from jax.sharding import PartitionSpec as P

FACTOR = 4
SUBSTEPS = 4

TIME_INCREMENT = 0.1
COUPLING = 3.0
PARTITION = 0.3
DIFFUSION = 1.0
THERMAL_SPREAD = 1.2
FREEZING_WARMTH = 2.0

LANES = 128
ROWS = 8
HALO = FACTOR * SUBSTEPS
BANDS = 4
SLOT = 2 * HALO
SMALL_VMEM = 4 << 20
STEP_VMEM = 24 << 20


def padded_2(cells, sides, width):
    for axis, dim in sides:
        count = lax.axis_size(axis)
        head = lax.slice_in_dim(cells, 0, width, axis=dim)
        tail = lax.slice_in_dim(cells, cells.shape[dim] - width, cells.shape[dim], axis=dim)
        cells = jnp.concatenate(
            [
                lax.ppermute(tail, axis, [(i, (i + 1) % count) for i in range(count)]),
                cells,
                lax.ppermute(head, axis, [((i + 1) % count, i) for i in range(count)]),
            ],
            axis=dim,
        )
    return cells


def laplace_padded(padded):
    center = padded[1:-1, 1:-1, 1:-1]
    total = padded[2:, 1:-1, 1:-1] + padded[:-2, 1:-1, 1:-1]
    total = total + padded[1:-1, 2:, 1:-1] + padded[1:-1, :-2, 1:-1]
    total = total + padded[1:-1, 1:-1, 2:] + padded[1:-1, 1:-1, :-2]
    return total - 6.0 * center


def flux_padded(values, mobility):
    center_v = values[1:-1, 1:-1, 1:-1]
    center_m = mobility[1:-1, 1:-1, 1:-1]
    total = jnp.zeros_like(center_v)
    pairs = (
        (
            values[2:, 1:-1, 1:-1],
            values[:-2, 1:-1, 1:-1],
            mobility[2:, 1:-1, 1:-1],
            mobility[:-2, 1:-1, 1:-1],
        ),
        (
            values[1:-1, 2:, 1:-1],
            values[1:-1, :-2, 1:-1],
            mobility[1:-1, 2:, 1:-1],
            mobility[1:-1, :-2, 1:-1],
        ),
        (
            values[1:-1, 1:-1, 2:],
            values[1:-1, 1:-1, :-2],
            mobility[1:-1, 1:-1, 2:],
            mobility[1:-1, 1:-1, :-2],
        ),
    )
    for upper_v, lower_v, upper_m, lower_m in pairs:
        total = (
            total
            + 0.5 * (upper_m + center_m) * (upper_v - center_v)
            - 0.5 * (center_m + lower_m) * (center_v - lower_v)
        )
    return total


def phase_update(phase_pad, centre_phase, centre_solute, centre_temp):
    square = 1.0 - centre_phase * centre_phase
    driving = (
        laplace_padded(phase_pad)
        + centre_phase
        - centre_phase * centre_phase * centre_phase
        - COUPLING * square * square * (centre_solute + centre_temp)
    )
    return jnp.clip(centre_phase + TIME_INCREMENT * driving, -1.0, 1.0)


def stepwise(order_parameter, dissolved_species, broad_undercool):
    size_x, size_y, size_z = order_parameter.shape
    coarse_x = size_x // FACTOR
    coarse_y = size_y // FACTOR
    coarse_z = size_z // FACTOR
    start_x = lax.axis_index("gx") * coarse_x
    own_block = lax.dynamic_slice_in_dim(broad_undercool, start_x, coarse_x, 2)
    for substep in range(SUBSTEPS):
        planes = own_block
        local_col = jnp.transpose(planes, (2, 0, 1))
        fine_temp = jnp.repeat(jnp.repeat(jnp.repeat(local_col, FACTOR, 0), FACTOR, 1), FACTOR, 2)
        stacked = jnp.stack([order_parameter, dissolved_species])
        padded = padded_2(stacked, (("gx", 1), ("gy", 2), ("gz", 3)), 1)
        solute_pad = padded[1]
        new_phase = phase_update(padded[0], order_parameter, dissolved_species, fine_temp)
        new_pad = padded_2(new_phase, (("gx", 0), ("gy", 1), ("gz", 2)), 1)
        mobility = 0.5 * (1.0 - new_pad)
        change = new_phase - order_parameter
        numer = (
            TIME_INCREMENT * DIFFUSION * flux_padded(solute_pad, mobility)
            + 0.5 * (1.0 + (1.0 - PARTITION) * dissolved_species) * change
        )
        new_solute = dissolved_species + numer / (
            0.5 * (1.0 + PARTITION - (1.0 - PARTITION) * new_phase)
        )
        blocks = (0.5 * change).reshape(coarse_x, FACTOR, coarse_y, FACTOR, coarse_z, FACTOR)
        freezing_warmth_source = jnp.transpose(jnp.mean(blocks, axis=(1, 3, 5)), (1, 2, 0))
        block_pad = padded_2(own_block, (("gx", 2), ("gy", 0), ("gz", 1)), 1)
        own_block = (
            own_block
            + TIME_INCREMENT * THERMAL_SPREAD * laplace_padded(block_pad)
            + FREEZING_WARMTH * freezing_warmth_source
        )
        order_parameter = new_phase
        dissolved_species = new_solute
    vertical_pile = lax.all_gather(own_block, "gx", axis=2, tiled=True)
    return (order_parameter, dissolved_species, vertical_pile)


def lane_index(shape):
    return lax.broadcasted_iota(jnp.int32, shape, 1)


def turn(tile, shift):
    shift = shift % LANES
    return tile if shift == 0 else pltpu.roll(tile, shift, 1)


def choose(pairs, shape, width):
    group = lane_index(shape) // width
    out = pairs[0][1]
    for index, tile in pairs[1:]:
        out = jnp.where(group == index, tile, out)
    return out


def spread_matrix(rows, cols, by_row):
    i = lax.broadcasted_iota(jnp.int32, (rows, cols), 0)
    j = lax.broadcasted_iota(jnp.int32, (rows, cols), 1)
    same = (i // FACTOR == j) if by_row else (i == j // FACTOR)
    return same.astype(jnp.float32)


def pick_matrix(rows, cols, by_row):
    i = lax.broadcasted_iota(jnp.int32, (rows, cols), 0)
    j = lax.broadcasted_iota(jnp.int32, (rows, cols), 1)
    same = (j == i * FACTOR) if by_row else (i == j * FACTOR)
    return same.astype(jnp.float32)


def exact_dot(a, b):
    return jnp.dot(a, b, precision=lax.Precision.HIGHEST, preferred_element_type=jnp.float32)


def pack_kernel(me_ref, p_ref, u_ref, t_ref, zlo, zhi, tf_ref):
    size_x, size_y, _ = p_ref.shape
    first = me_ref[0] == 0
    wide = spread_matrix(size_y, t_ref.shape[0], True)
    long = spread_matrix(t_ref.shape[2], LANES, False)
    layers = [exact_dot(exact_dot(wide, t_ref[:, g, :]), long) for g in range(2)]
    for g in range(2):
        tf_ref[g] = jnp.where(first, layers[g], layers[1 - g])
    sources = [p_ref.at[i] for i in range(size_x)] + [u_ref.at[i] for i in range(size_x)] + [tf_ref.at[g] for g in range(2)]
    shape = (HALO, LANES)
    parts = size_y // HALO
    for i, src in enumerate(sources):
        rows = [src[pl.ds(HALO * g, HALO), :] for g in range(parts)]
        zlo[i] = choose([(g, turn(rows[g], HALO * g)) for g in range(parts)], shape, HALO)
        zhi[i] = choose([(g, turn(rows[g], HALO * g + HALO)) for g in range(parts)], shape, HALO)


def band_shape(size_y):
    tall = size_y + 2 * HALO
    return tall // BANDS, BANDS * tall // LANES


def side_kernel(p_ref, u_ref, tf_ref, zlo, zhi, side, side_t, ylo, yhi):
    size_x, size_y, _ = p_ref.shape
    band, _ = band_shape(size_y)
    shape = (ROWS, LANES)
    fields = 2 * size_x
    for f in range(fields + 2):
        out = side.at[f] if f < fields else side_t.at[f - fields]
        for r in range(0, band, ROWS):
            pairs = []
            for b in range(BANDS):
                y = band * b + r - HALO
                if 0 <= y < size_y:
                    j, sub = divmod(y, HALO)
                    rows = pl.ds(sub, ROWS)
                    pairs.append((2 * b, turn(zlo[f, rows, :], SLOT * b - HALO * j)))
                    pairs.append((2 * b + 1, turn(zhi[f, rows, :], SLOT * b + HALO - HALO * j)))
            out[pl.ds(r, ROWS), :] = choose(pairs, shape, HALO)
    shape = (HALO, LANES)
    for out, y, b in ((ylo, 0, 0), (yhi, size_y - HALO, BANDS - 1)):
        r = y + HALO - band * b
        for f in range(fields):
            out[f] = (p_ref if f < size_x else u_ref)[f % size_x, pl.ds(y, HALO), :]
        for field in range(2):
            tiles = [(k, turn(side[field * size_x + k, pl.ds(r, HALO), :], SLOT * (k - b))) for k in range(size_x)]
            out[fields + field] = choose(tiles, shape, SLOT)
        few = HALO // FACTOR
        for g in range(2):
            out[fields + 2, pl.ds(few * g, few), :] = tf_ref[g, pl.ds(y, few, stride=FACTOR), :]
        tiles = [(g, turn(side_t[g, pl.ds(r, few, stride=FACTOR), :], SLOT * (g - b))) for g in range(2)]
        out[fields + 2, pl.ds(2 * few, few), :] = choose(tiles, (few, LANES), SLOT)
        out[fields + 2, pl.ds(3 * few, few), :] = jnp.zeros((few, LANES), jnp.float32)


def step_kernel(
    me_ref, p_ref, u_ref, tf_ref, pp_ref, up_ref, side, side_t, ylo, yhi, side_other, ylo_other, yhi_other,
    po_ref, uo_ref, to_ref,
    p0, p1, u0, u1, around, p_up, p_down, u_up, u_down, warm, heats, k0, k1, flat,
):
    size_x, size_y, _ = p_ref.shape
    planes = 2 * size_x
    band, tiles = band_shape(size_y)
    shape = (ROWS, LANES)
    lane = lane_index(shape)
    row = lax.broadcasted_iota(jnp.int32, shape, 0)
    phase, solute, coarse = (p0, p1), (u0, u1), (k0, k1)
    top = ROWS
    few = band // FACTOR
    every = range(tiles)

    def to_bands(rows_of, halo):
        turned = [turn(rows_of(b), HALO + SLOT * b) for b in range(BANDS)]
        out = []
        for t in every:
            tile = halo
            if t > 0:
                tile = jnp.where(lane < SLOT * t - HALO, turned[t - 1], tile)
            if t < BANDS:
                tile = jnp.where(lane >= SLOT * t + HALO, turned[t], tile)
            out.append(tile)
        return out

    def from_bands(tile_of, b):
        at = HALO + SLOT * b
        return turn(jnp.where(lane_index(tile_of(b).shape) >= at, tile_of(b), tile_of(b + 1)), -at)

    def row_source(core, low, high):
        def rows_of(b, r):
            y = band * b + r - HALO
            return low(r) if y < 0 else high(y - size_y) if y >= size_y else core(y)

        return rows_of

    for field, (dst, own, other) in enumerate(((p0, p_ref, pp_ref), (u0, u_ref, up_ref))):
        for g, (core, lo, hi, sides) in enumerate(((own, ylo, yhi, side), (other, ylo_other, yhi_other, side_other))):
            for k in range(size_x):
                f = field * size_x + k
                rows_of = row_source(
                    lambda y: core[k, pl.ds(y, ROWS), :],
                    lambda r: lo[f, pl.ds(r, ROWS), :],
                    lambda r: hi[f, pl.ds(r, ROWS), :],
                )
                for r in range(0, band, ROWS):
                    halo = sides[f, pl.ds(r, ROWS), :]
                    if r < HALO:
                        halo = jnp.where(lane < SLOT, turn(lo[planes + field, pl.ds(r, ROWS), :], -SLOT * k), halo)
                    if r >= band - HALO:
                        corner = hi[planes + field, pl.ds(r - band + HALO, ROWS), :]
                        halo = jnp.where(lane >= LANES - SLOT, turn(corner, -SLOT - SLOT * k), halo)
                    for t, tile in enumerate(to_bands(lambda b: rows_of(b, r), halo)):
                        dst[g * size_x + k, t, pl.ds(top + r, ROWS), :] = tile
    for g in range(2):
        def spread(ref, first, r):
            at = first + r // FACTOR
            return jnp.where(row < FACTOR, ref[planes + 2, pl.ds(at, 1), :], ref[planes + 2, pl.ds(at + 1, 1), :])

        rows_of = row_source(
            lambda y: tf_ref[g, pl.ds(y, ROWS), :],
            lambda r: spread(ylo, HALO // FACTOR * g, r),
            lambda r: spread(yhi, HALO // FACTOR * g, r),
        )
        for r in range(0, band, ROWS):
            halo = side_t[g, pl.ds(r, ROWS), :]
            if r < HALO:
                halo = jnp.where(lane < SLOT, turn(spread(ylo, 2 * HALO // FACTOR, r), -SLOT * g), halo)
            if r >= band - HALO:
                corner = spread(yhi, 2 * HALO // FACTOR, r - band + HALO)
                halo = jnp.where(lane >= LANES - SLOT, turn(corner, -SLOT - SLOT * g), halo)
            for t, tile in enumerate(to_bands(lambda b: rows_of(b, r), halo)):
                warm[g, t, pl.ds(r, ROWS), :] = tile
        for t in every:
            k0[g, t, pl.ds(top, few), :] = warm[g, t, pl.ds(0, few, stride=FACTOR), :]

    def along_z(cells, reach):
        left = [turn(c, -reach) for c in cells]
        right = [turn(c, reach) for c in cells]
        up = [jnp.where(lane >= LANES - reach, left[t + 1], left[t]) if t + 1 < tiles else left[t] for t in every]
        down = [jnp.where(lane < reach, right[t - 1], right[t]) if t > 0 else right[t] for t in every]
        return up, down

    def keep_shifts(field, up, down, at, some):
        for k in some:
            above, below = along_z([field[k, t, pl.ds(at, ROWS), :] for t in every], 1)
            for t in every:
                up[k, t, pl.ds(at, ROWS), :] = above[t]
                down[k, t, pl.ds(at, ROWS), :] = below[t]

    def join_bands(field, some, rows):
        for k in some:
            last = [turn(field[k, t, pl.ds(top + rows - ROWS, ROWS), :], SLOT) for t in every]
            start = [turn(field[k, t, pl.ds(top, ROWS), :], -SLOT) for t in every]
            for t in every:
                if t > 0:
                    tile = last[t - 1] if t == 1 else jnp.where(lane >= SLOT, last[t - 1], last[t - 2])
                    field[k, t, pl.ds(top - ROWS, ROWS), :] = tile
                if t + 1 < tiles:
                    tile = start[t + 1] if t + 2 == tiles else jnp.where(lane < LANES - SLOT, start[t + 1], start[t + 2])
                    field[k, t, pl.ds(top + rows, ROWS), :] = tile

    def sweep(work, follow):
        def body(i, _):
            at = pl.multiple_of(top + i * ROWS, ROWS)
            if follow is not None:
                follow(at - ROWS)
            work(at)

        lax.fori_loop(0, band // ROWS, body, None)
        if follow is not None:
            follow(top + band - ROWS)

    def new_value(c, total, drive):
        c2 = c * c
        square = 1.0 - c2
        driving = total - c * (5.0 + c2) - (COUPLING * square * square) * drive
        return jnp.clip(c + TIME_INCREMENT * driving, -1.0, 1.0)

    def phase_pass(step, kept):
        pa, pb, ua = phase[step % 2], phase[(step + 1) % 2], solute[step % 2]

        def work(at):
            here, above, below = pl.ds(at, ROWS), pl.ds(at + 1, ROWS), pl.ds(at - 1, ROWS)
            plain = pl.ds(at - top, ROWS)
            for g in range(2):
                for t in every:
                    heat = None
                    temperature = warm[g, t, plain, :]
                    for k in range(g * size_x, (g + 1) * size_x):
                        old = pa[k, t, here, :]
                        if step == 0:
                            total = pa[(k + 1) % planes, t, here, :] + pa[(k - 1) % planes, t, here, :]
                            total = total + pa[k, t, above, :] + pa[k, t, below, :]
                            total = total + p_up[k, t, here, :] + p_down[k, t, here, :]
                        else:
                            total = around[k, t, here, :]
                        new = new_value(old, total, ua[k, t, here, :] + temperature)
                        pb[k, t, here, :] = new
                        heat = new - old if heat is None else heat + (new - old)
                    heats[g, t, plain, :] = heat

        sweep(work, lambda at: keep_shifts(pb, p_up, p_down, at, kept))
        join_bands(pb, kept, band)

    def temperature_pass(step, last):
        ka, kb = coarse[step % 2], coarse[(step + 1) % 2]
        scale = FREEZING_WARMTH * 0.5 / FACTOR**3
        conduct = TIME_INCREMENT * THERMAL_SPREAD
        place = lane % FACTOR

        def pooled(v):
            out = v
            for by in range(1, FACTOR):
                out = out + jnp.where(place < FACTOR - by, turn(v, -by), turn(v, FACTOR - by))
            return out

        for g in range(2):
            for r in range(0, few, ROWS):
                count = min(ROWS, few - r)
                at = pl.ds(top + r, ROWS)
                far, near = pl.ds(top + r + 1, ROWS), pl.ds(top + r - 1, ROWS)
                up, down = along_z([ka[g, t, at, :] for t in every], FACTOR)
                for t in every:
                    heat = sum(heats[g, t, pl.ds(FACTOR * r + j, ROWS, stride=FACTOR), :] for j in range(FACTOR))
                    mine = ka[g, t, at, :]
                    total = 2.0 * ka[1 - g, t, at, :] + up[t] + down[t] + ka[g, t, far, :] + ka[g, t, near, :]
                    new = mine + conduct * (total - 6.0 * mine) + scale * pooled(heat)
                    kb[g, t, at, :] = new
                    if not last:
                        for j in range(FACTOR):
                            warm[g, t, pl.ds(FACTOR * r + j, count, stride=FACTOR), :] = new[:count]
        if not last:
            join_bands(kb, range(2), few)

    def solute_pass(step, last):
        pa, pb = phase[step % 2], phase[(step + 1) % 2]
        ua, ub = solute[step % 2], solute[(step + 1) % 2]

        def cell(u, p, p_old, near, zs):
            total_u = near[0][0] + near[1][0] + near[2][0] + near[3][0]
            total_p = near[0][1] + near[1][1] + near[2][1] + near[3][1]
            total_w = near[0][0] * near[0][1] + near[1][0] * near[1][1] + near[2][0] * near[2][1] + near[3][0] * near[3][1]
            p2 = 2.0 - p
            flux = p2 * (total_u - 4.0 * u) + u * total_p - total_w
            for zu, zp in zs:
                flux = flux + (p2 - zp) * (zu - u)
            change = p - p_old
            numer = (0.25 * TIME_INCREMENT * DIFFUSION) * flux + (0.5 + 0.5 * (1.0 - PARTITION) * u) * change
            new = u + numer / (0.5 * (1.0 + PARTITION) - 0.5 * (1.0 - PARTITION) * p)
            return new, total_p + zs[0][1] + zs[1][1]

        def work(at):
            here, above, below = pl.ds(at, ROWS), pl.ds(at + 1, ROWS), pl.ds(at - 1, ROWS)
            for t in every:
                for k in range(size_x if last else planes):
                    pick = lambda i, w: (ua[i % planes, t, w, :], pb[i % planes, t, w, :])
                    near = [pick(k + 1, here), pick(k - 1, here), pick(k, above), pick(k, below)]
                    zs = [(u_up[k, t, here, :], p_up[k, t, here, :]), (u_down[k, t, here, :], p_down[k, t, here, :])]
                    u, p = pick(k, here)
                    new, total = cell(u, p, pa[k, t, here, :], near, zs)
                    ub[k, t, here, :] = new
                    if not last:
                        around[k, t, here, :] = total

        everything = range(planes)
        sweep(work, None if last else lambda at: keep_shifts(ub, u_up, u_down, at, everything))
        if not last:
            join_bands(ub, everything, band)

    everything, own = range(planes), range(size_x)

    def first_shifts(at):
        keep_shifts(p0, p_up, p_down, at, everything)
        keep_shifts(u0, u_up, u_down, at, everything)

    sweep(first_shifts, None)
    join_bands(p0, everything, band)
    join_bands(u0, everything, band)
    join_bands(k0, range(2), few)
    for step in range(SUBSTEPS):
        last = step == SUBSTEPS - 1
        phase_pass(step, own if last else everything)
        temperature_pass(step, last)
        solute_pass(step, last)

    for src, out in ((phase[SUBSTEPS % 2], po_ref), (solute[SUBSTEPS % 2], uo_ref)):
        for k in own:
            for r in range(0, band, ROWS):
                for b in range(BANDS):
                    y = band * b + r - HALO
                    if 0 <= y < size_y:
                        out[k, pl.ds(y, ROWS), :] = from_bands(lambda t: src[k, t, pl.ds(top + r, ROWS), :], b)
    first = me_ref[0] == 0
    short = pick_matrix(LANES, to_ref.shape[2], False)
    last = coarse[SUBSTEPS % 2]
    layers = []
    for g in range(2):
        for b in range(BANDS):
            flat[g, pl.ds(ROWS + few * b - HALO // FACTOR, 2 * ROWS), :] = from_bands(lambda t: last[g, t, pl.ds(top, 2 * ROWS), :], b)
        layers.append(exact_dot(flat[g, pl.ds(ROWS, to_ref.shape[0]), :], short))
    for g in range(2):
        to_ref[:, g, :] = jnp.where(first, layers[g], layers[1 - g])


def shifted(x, axis, step):
    count = lax.axis_size(axis)
    return lax.ppermute(x, axis, [(i, (i + step) % count) for i in range(count)])


def swapped(x):
    return lax.ppermute(x, "gx", [(0, 1), (1, 0)])


def at_once(order_parameter, dissolved_species, broad_undercool):
    size_x, size_y, size_z = order_parameter.shape
    f32 = jnp.float32
    planes = 2 * size_x
    me = lax.axis_index("gx").astype(jnp.int32).reshape(1)
    coarse = jnp.transpose(broad_undercool, (0, 2, 1))
    smem = pl.BlockSpec(memory_space=pltpu.SMEM)
    vmem = pl.BlockSpec(memory_space=pltpu.VMEM)
    shape = jax.ShapeDtypeStruct
    band, tiles = band_shape(size_y)
    small = pltpu.CompilerParams(vmem_limit_bytes=SMALL_VMEM)

    partner_p = swapped(order_parameter)
    partner_u = swapped(dissolved_species)

    strip = shape((planes + 2, HALO, LANES), f32)
    to_low, to_high, fine = pl.pallas_call(
        pack_kernel,
        out_shape=[strip] * 2 + [shape((2, size_y, size_z), f32)],
        in_specs=[smem, vmem, vmem, vmem],
        out_specs=[vmem] * 3,
        compiler_params=small,
        name="pack",
    )(me, order_parameter, dissolved_species, coarse)
    zhi, zlo = shifted(to_low, "gz", -1), shifted(to_high, "gz", 1)
    strip = shape((planes + 3, HALO, LANES), f32)
    side, side_t, to_low, to_high = pl.pallas_call(
        side_kernel,
        out_shape=[shape((planes, band, LANES), f32), shape((2, band, LANES), f32), strip, strip],
        in_specs=[vmem] * 5,
        out_specs=[vmem] * 4,
        compiler_params=small,
        name="side",
    )(order_parameter, dissolved_species, fine, zlo, zhi)
    side_other = swapped(side)
    yhi, ylo = shifted(to_low, "gy", -1), shifted(to_high, "gy", 1)
    ylo_other, yhi_other = swapped(ylo), swapped(yhi)

    cells = pltpu.VMEM((planes, tiles, band + 2 * ROWS, LANES), f32)
    warm = pltpu.VMEM((2, tiles, band + 3 * ROWS, LANES), f32)
    flat = pltpu.VMEM((2, size_y // FACTOR + 3 * ROWS, LANES), f32)
    new_p, new_u, new_t = pl.pallas_call(
        step_kernel,
        out_shape=[shape(order_parameter.shape, f32), shape(dissolved_species.shape, f32), shape(coarse.shape, f32)],
        in_specs=[smem] + [vmem] * 12,
        out_specs=[vmem] * 3,
        scratch_shapes=[cells] * 9 + [warm] * 2 + [warm] * 2 + [flat],
        compiler_params=pltpu.CompilerParams(vmem_limit_bytes=STEP_VMEM),
        name="steps",
    )(
        me, order_parameter, dissolved_species, fine, partner_p, partner_u,
        side, side_t, ylo, yhi, side_other, ylo_other, yhi_other,
    )
    return new_p, new_u, jnp.transpose(new_t, (0, 2, 1))


def per_device(order_parameter, dissolved_species, broad_undercool):
    size_x, size_y, size_z = order_parameter.shape
    whole_x = lax.axis_size("gx") == 2 and broad_undercool.shape[2] * FACTOR == 2 * size_x
    if whole_x and size_x == FACTOR == BANDS and size_y == size_z == LANES == SLOT * BANDS:
        return at_once(order_parameter, dissolved_species, broad_undercool)
    return stepwise(order_parameter, dissolved_species, broad_undercool)


def solution(mesh):
    return jax.shard_map(
        per_device,
        mesh=mesh,
        in_specs=(P("gx", "gy", "gz"), P("gx", "gy", "gz"), P("gy", "gz", None)),
        out_specs=(P("gx", "gy", "gz"), P("gx", "gy", "gz"), P("gy", "gz", None)),
        check_vma=False,
    )
```

```python
import jax
import jax.numpy as jnp
from jax import lax
from jax.experimental import pallas as pl
from jax.experimental.pallas import tpu as pltpu
from jax.sharding import PartitionSpec as P


FACTOR = 4
SUBSTEPS = 4

TIME_INCREMENT = 0.1
COUPLING = 3.0
PARTITION = 0.3
DIFFUSION = 1.0
THERMAL_SPREAD = 1.2
FREEZING_WARMTH = 2.0

LANES = 128
ROWS = 8
HALO = FACTOR * SUBSTEPS
BANDS = 4
SLOT = 2 * HALO
REACH_P = HALO - FACTOR + 1
REACH_U = HALO - FACTOR
SMALL_VMEM = 4 << 20
STEP_VMEM = 24 << 20


def padded_2(cells, sides, width):
    for axis, dim in sides:
        count = lax.axis_size(axis)
        head = lax.slice_in_dim(cells, 0, width, axis=dim)
        tail = lax.slice_in_dim(cells, cells.shape[dim] - width, cells.shape[dim], axis=dim)
        cells = jnp.concatenate(
            [
                lax.ppermute(tail, axis, [(i, (i + 1) % count) for i in range(count)]),
                cells,
                lax.ppermute(head, axis, [((i + 1) % count, i) for i in range(count)]),
            ],
            axis=dim,
        )
    return cells


def laplace_padded(padded):
    center = padded[1:-1, 1:-1, 1:-1]
    total = padded[2:, 1:-1, 1:-1] + padded[:-2, 1:-1, 1:-1]
    total = total + padded[1:-1, 2:, 1:-1] + padded[1:-1, :-2, 1:-1]
    total = total + padded[1:-1, 1:-1, 2:] + padded[1:-1, 1:-1, :-2]
    return total - 6.0 * center


def flux_padded(values, mobility):
    center_v = values[1:-1, 1:-1, 1:-1]
    center_m = mobility[1:-1, 1:-1, 1:-1]
    total = jnp.zeros_like(center_v)
    pairs = (
        (
            values[2:, 1:-1, 1:-1],
            values[:-2, 1:-1, 1:-1],
            mobility[2:, 1:-1, 1:-1],
            mobility[:-2, 1:-1, 1:-1],
        ),
        (
            values[1:-1, 2:, 1:-1],
            values[1:-1, :-2, 1:-1],
            mobility[1:-1, 2:, 1:-1],
            mobility[1:-1, :-2, 1:-1],
        ),
        (
            values[1:-1, 1:-1, 2:],
            values[1:-1, 1:-1, :-2],
            mobility[1:-1, 1:-1, 2:],
            mobility[1:-1, 1:-1, :-2],
        ),
    )
    for upper_v, lower_v, upper_m, lower_m in pairs:
        total = (
            total
            + 0.5 * (upper_m + center_m) * (upper_v - center_v)
            - 0.5 * (center_m + lower_m) * (center_v - lower_v)
        )
    return total


def phase_update(phase_pad, centre_phase, centre_solute, centre_temp):
    square = 1.0 - centre_phase * centre_phase
    driving = (
        laplace_padded(phase_pad)
        + centre_phase
        - centre_phase * centre_phase * centre_phase
        - COUPLING * square * square * (centre_solute + centre_temp)
    )
    return jnp.clip(centre_phase + TIME_INCREMENT * driving, -1.0, 1.0)


def stepwise(order_parameter, dissolved_species, broad_undercool):
    size_x, size_y, size_z = order_parameter.shape
    coarse_x = size_x // FACTOR
    coarse_y = size_y // FACTOR
    coarse_z = size_z // FACTOR
    start_x = lax.axis_index("gx") * coarse_x
    own_block = lax.dynamic_slice_in_dim(broad_undercool, start_x, coarse_x, 2)
    for _ in range(SUBSTEPS):
        planes = own_block
        local_col = jnp.transpose(planes, (2, 0, 1))
        fine_temp = jnp.repeat(jnp.repeat(jnp.repeat(local_col, FACTOR, 0), FACTOR, 1), FACTOR, 2)
        stacked = jnp.stack([order_parameter, dissolved_species])
        padded = padded_2(stacked, (("gx", 1), ("gy", 2), ("gz", 3)), 1)
        solute_pad = padded[1]
        new_phase = phase_update(padded[0], order_parameter, dissolved_species, fine_temp)
        new_pad = padded_2(new_phase, (("gx", 0), ("gy", 1), ("gz", 2)), 1)
        mobility = 0.5 * (1.0 - new_pad)
        change = new_phase - order_parameter
        numer = (
            TIME_INCREMENT * DIFFUSION * flux_padded(solute_pad, mobility)
            + 0.5 * (1.0 + (1.0 - PARTITION) * dissolved_species) * change
        )
        new_solute = dissolved_species + numer / (
            0.5 * (1.0 + PARTITION - (1.0 - PARTITION) * new_phase)
        )
        blocks = (0.5 * change).reshape(coarse_x, FACTOR, coarse_y, FACTOR, coarse_z, FACTOR)
        freezing_warmth_source = jnp.transpose(jnp.mean(blocks, axis=(1, 3, 5)), (1, 2, 0))
        block_pad = padded_2(own_block, (("gx", 2), ("gy", 0), ("gz", 1)), 1)
        own_block = (
            own_block
            + TIME_INCREMENT * THERMAL_SPREAD * laplace_padded(block_pad)
            + FREEZING_WARMTH * freezing_warmth_source
        )
        order_parameter = new_phase
        dissolved_species = new_solute
    vertical_pile = lax.all_gather(own_block, "gx", axis=2, tiled=True)
    return (order_parameter, dissolved_species, vertical_pile)


def lane_index(shape):
    return lax.broadcasted_iota(jnp.int32, shape, 1)


def turn(tile, shift):
    shift = shift % LANES
    return tile if shift == 0 else pltpu.roll(tile, shift, 1)


def choose(pairs, shape, width):
    group = lane_index(shape) // width
    out = pairs[0][1]
    for index, tile in pairs[1:]:
        out = jnp.where(group == index, tile, out)
    return out


def spread_matrix(rows, cols, by_row):
    i = lax.broadcasted_iota(jnp.int32, (rows, cols), 0)
    j = lax.broadcasted_iota(jnp.int32, (rows, cols), 1)
    same = (i // FACTOR == j) if by_row else (i == j // FACTOR)
    return same.astype(jnp.float32)


def pick_matrix(rows, cols, by_row):
    i = lax.broadcasted_iota(jnp.int32, (rows, cols), 0)
    j = lax.broadcasted_iota(jnp.int32, (rows, cols), 1)
    same = (j == i * FACTOR) if by_row else (i == j * FACTOR)
    return same.astype(jnp.float32)


def exact_dot(a, b):
    return jnp.dot(a, b, precision=lax.Precision.HIGHEST, preferred_element_type=jnp.float32)


def pool_lanes(v):
    i = lax.broadcasted_iota(jnp.int32, (LANES, LANES), 0)
    j = lax.broadcasted_iota(jnp.int32, (LANES, LANES), 1)
    same = (i // FACTOR == j // FACTOR).astype(jnp.float32).astype(jnp.bfloat16)
    total = None
    for _ in range(3):
        part = v.astype(jnp.bfloat16)
        v = v - part.astype(jnp.float32)
        term = jnp.dot(part, same, preferred_element_type=jnp.float32)
        total = term if total is None else total + term
    return total


def pack_kernel(me_ref, p_hbm, u_hbm, t_hbm, zlo, zhi, tf_ref, p_ref, u_ref, t_ref, sems):
    size_x, size_y, _ = p_ref.shape
    pairs = ((t_hbm, t_ref), (p_hbm, p_ref), (u_hbm, u_ref))
    copies = [pltpu.make_async_copy(src, dst, sems.at[i]) for i, (src, dst) in enumerate(pairs)]
    for copy in copies:
        copy.start()
    copies[0].wait()
    first = me_ref[0] == 0
    long = spread_matrix(t_ref.shape[2], LANES, False)
    layers = exact_dot(jnp.concatenate([t_ref[:, g, :] for g in range(2)], 0), long)
    count = t_ref.shape[0]
    layers = [layers[count * g : count * g + count] for g in range(2)]
    for g in range(2):
        layer = jnp.where(first, layers[g], layers[1 - g])
        for j in range(FACTOR):
            tf_ref[g, pl.ds(j, count, stride=FACTOR), :] = layer
    shape = (HALO, LANES)
    parts = size_y // HALO

    def strips(ref, at):
        for i in range(ref.shape[0]):
            rows = [ref[i, pl.ds(HALO * g, HALO), :] for g in range(parts)]
            zlo[at + i] = choose([(g, turn(rows[g], HALO * g)) for g in range(parts)], shape, HALO)
            zhi[at + i] = choose([(g, turn(rows[g], HALO * g + HALO)) for g in range(parts)], shape, HALO)

    strips(tf_ref, 2 * size_x)
    copies[1].wait()
    strips(p_ref, 0)
    copies[2].wait()
    strips(u_ref, size_x)


def band_shape(size_y):
    tall = size_y + 2 * HALO
    return tall // BANDS, BANDS * tall // LANES


def side_kernel(p_ref, u_ref, tf_ref, zlo, zhi, side, side_t, ylo, yhi):
    size_x, size_y, _ = p_ref.shape
    band, _ = band_shape(size_y)
    shape = (ROWS, LANES)
    fields = 2 * size_x
    for f in range(fields + 2):
        out = side.at[f] if f < fields else side_t.at[f - fields]
        for r in range(0, band, ROWS):
            pairs = []
            for b in range(BANDS):
                y = band * b + r - HALO
                if 0 <= y < size_y:
                    j, sub = divmod(y, HALO)
                    rows = pl.ds(sub, ROWS)
                    pairs.append((2 * b, turn(zlo[f, rows, :], SLOT * b - HALO * j)))
                    pairs.append((2 * b + 1, turn(zhi[f, rows, :], SLOT * b + HALO - HALO * j)))
            out[pl.ds(r, ROWS), :] = choose(pairs, shape, HALO)
    for out, y, b, below in ((ylo, 0, 0, True), (yhi, size_y, BANDS - 1, False)):
        for field, ref in enumerate((p_ref, u_ref)):
            reach, at = strip_rows(size_x, field, 0)
            first = y if below else y - reach
            r = first + HALO - band * b
            for k in range(size_x):
                out[pl.ds(at + reach * k, reach), :] = ref[k, pl.ds(first, reach), :]
            tiles = [(k, turn(side[field * size_x + k, pl.ds(r, reach), :], SLOT * (k - b))) for k in range(size_x)]
            out[pl.ds(at + reach * size_x, reach), :] = choose(tiles, (reach, LANES), SLOT)
        few = HALO // FACTOR
        _, at = strip_rows(size_x, 2, 0)
        first = y if below else y - HALO
        r = first + HALO - band * b
        for g in range(2):
            out[pl.ds(at + few * g, few), :] = tf_ref[g, pl.ds(first, few, stride=FACTOR), :]
        tiles = [(g, turn(side_t[g, pl.ds(r, few, stride=FACTOR), :], SLOT * (g - b))) for g in range(2)]
        out[pl.ds(at + 2 * few, few), :] = choose(tiles, (few, LANES), SLOT)


def strip_rows(size_x, field, tile):
    reach = (REACH_P, REACH_U, HALO // FACTOR)[field]
    return reach, HALO - REACH_P + (size_x + 1) * sum((REACH_P, REACH_U)[:field]) + reach * tile


def strip_height(size_x):
    rows = strip_rows(size_x, 2, 3)[1]
    return -(-rows // ROWS) * ROWS


def strip_readers(size_x, field, tile, low_ref, high_ref):
    reach, at = strip_rows(size_x, field, tile)

    def low(r):
        return low_ref[pl.ds(at + r - (HALO - reach), ROWS), :]

    def high(r):
        return high_ref[pl.ds(at + r, ROWS), :]

    return low, high


def to_bands(rows_of, halo, tiles):
    lane = lane_index((ROWS, LANES))
    turned = [turn(rows_of(b), HALO + SLOT * b) for b in range(BANDS)]
    out = []
    for t in range(tiles):
        tile = halo
        if t > 0:
            tile = jnp.where(lane < SLOT * t - HALO, turned[t - 1], tile)
        if t < BANDS:
            tile = jnp.where(lane >= SLOT * t + HALO, turned[t], tile)
        out.append(tile)
    return out


def fill_plane(put, core, low, high, side, corner_low, corner_high, slot, size_y):
    band, tiles = band_shape(size_y)
    lane = lane_index((ROWS, LANES))

    for r in range(0, band, ROWS):
        def rows_of(b):
            y = band * b + r - HALO
            return low(r) if y < 0 else high(y - size_y) if y >= size_y else core(y)

        halo = side(r)
        if r < HALO:
            halo = jnp.where(lane < SLOT, turn(corner_low(r), -SLOT * slot), halo)
        if r >= band - HALO:
            halo = jnp.where(lane >= LANES - SLOT, turn(corner_high(r - band + HALO), -SLOT - SLOT * slot), halo)
        for t, tile in enumerate(to_bands(rows_of, halo, tiles)):
            put(t, r, tile)


def along_z(cells, reach):
    lane = lane_index(cells[0].shape)
    tiles = len(cells)
    left = [turn(c, -reach) for c in cells]
    right = [turn(c, reach) for c in cells]
    up = [jnp.where(lane >= LANES - reach, left[t + 1], left[t]) if t + 1 < tiles else left[t] for t in range(tiles)]
    down = [jnp.where(lane < reach, right[t - 1], right[t]) if t > 0 else right[t] for t in range(tiles)]
    return up, down


def keep_shifts(field, up, down, at, some):
    tiles = field.shape[1]
    for k in some:
        above, below = along_z([field[k, t, pl.ds(at, ROWS), :] for t in range(tiles)], 1)
        for t in range(tiles):
            up[k, t, pl.ds(at, ROWS), :] = above[t]
            down[k, t, pl.ds(at, ROWS), :] = below[t]


def join_bands(field, some, rows):
    _, tiles, height, _ = field.shape
    flat = field.reshape(field.shape[0] * tiles * height, LANES)
    lane = lane_index((len(some), LANES))

    def row_of_planes(t, i):
        return pl.ds((some[0] * tiles + t) * height + i, len(some), stride=tiles * height)

    last = [turn(flat[row_of_planes(t, ROWS + rows - 1), :], SLOT) for t in range(tiles)]
    start = [turn(flat[row_of_planes(t, ROWS), :], -SLOT) for t in range(tiles)]
    for t in range(tiles):
        if t > 0:
            tile = last[t - 1] if t == 1 else jnp.where(lane >= SLOT, last[t - 1], last[t - 2])
            flat[row_of_planes(t, ROWS - 1), :] = tile
        if t + 1 < tiles:
            tile = start[t + 1] if t + 2 == tiles else jnp.where(lane < LANES - SLOT, start[t + 1], start[t + 2])
            flat[row_of_planes(t, ROWS + rows), :] = tile


def sweep(rows, work, follow=None, lead=None):
    if lead is not None:
        lead(ROWS)

    def body(i, _):
        at = pl.multiple_of(ROWS + i * ROWS, ROWS)
        if lead is not None:
            lead(at + ROWS)
        if follow is not None:
            follow(at - ROWS)
        work(at)

    lax.fori_loop(0, rows // ROWS, body, None)
    if follow is not None:
        follow(rows)


def own_kernel(p_ref, u_ref, tf_ref, side, side_t, ylo, yhi, p_own, u_own, p_up, p_down, u_up, u_down, warm, small):
    size_x, size_y, _ = p_ref.shape
    band, tiles = band_shape(size_y)
    few = band // FACTOR
    row = lax.broadcasted_iota(jnp.int32, (ROWS, LANES), 0)
    for field, (dst, core) in enumerate(((p_own, p_ref), (u_own, u_ref))):
        for k in range(size_x):
            f = field * size_x + k

            def put(t, r, tile):
                dst[k, t, pl.ds(ROWS + r, ROWS), :] = tile

            rows = strip_readers(size_x, field, k, ylo, yhi)
            corners = strip_readers(size_x, field, size_x, ylo, yhi)
            fill_plane(
                put, lambda y: core[k, pl.ds(y, ROWS), :], *rows, lambda r: side[f, pl.ds(r, ROWS), :], *corners, k, size_y
            )

    def spread(ref, part, r):
        at = strip_rows(size_x, 2, part)[1] + r // FACTOR
        return jnp.where(row < FACTOR, ref[pl.ds(at, 1), :], ref[pl.ds(at + 1, 1), :])

    for g in range(2):
        def put(t, r, tile):
            warm[g, t, pl.ds(r, ROWS), :] = tile

        fill_plane(
            put, lambda y: tf_ref[g, pl.ds(y, ROWS), :],
            lambda r: spread(ylo, g, r), lambda r: spread(yhi, g, r),
            lambda r: side_t[g, pl.ds(r, ROWS), :],
            lambda r: spread(ylo, 2, r), lambda r: spread(yhi, 2, r),
            g, size_y,
        )
        for t in range(tiles):
            small[g, t, pl.ds(ROWS, few), :] = warm[g, t, pl.ds(0, few, stride=FACTOR), :]
    own = range(size_x)

    def shifts(at):
        keep_shifts(p_own, p_up, p_down, at, own)
        keep_shifts(u_own, u_up, u_down, at, own)

    sweep(band, shifts)
    join_bands(p_own, own, band)
    join_bands(u_own, own, band)
    join_bands(small, range(2), few)


def step_kernel(
    me_ref, pp_ref, up_ref, side, ylo, yhi, p_own, u_own, p_up_own, p_down_own, u_up_own, u_down_own, warm_own, small_own,
    po_ref, uo_ref, to_ref,
    p0, p1, u0, u1, around, p_up, p_down, u_up, u_down, warm, heats, k0, k1, flat,
):
    size_x, size_y, _ = pp_ref.shape
    planes = 2 * size_x
    band, tiles = band_shape(size_y)
    shape = (ROWS, LANES)
    lane = lane_index(shape)
    few = band // FACTOR
    every = range(tiles)
    everything, own, others = range(planes), range(size_x), range(size_x, planes)

    def of_planes(mine, ref):
        return [mine.at[k] for k in own] + [ref.at[k] for k in others]

    def all_of(ref):
        return [ref.at[k] for k in everything]

    phase = [of_planes(p_own, p0), all_of(p1), all_of(p0)]
    solute = [of_planes(u_own, u0), all_of(u1), all_of(u0)]
    first_p_up, first_p_down = of_planes(p_up_own, p_up), of_planes(p_down_own, p_down)
    first_u_up, first_u_down = of_planes(u_up_own, u_up), of_planes(u_down_own, u_down)

    def at_step(states, step):
        return states[0] if step == 0 else states[2 - step % 2]

    for field, (dst, core) in enumerate(((p0, pp_ref), (u0, up_ref))):
        for k in range(size_x):
            f = field * size_x + k

            def put(t, r, tile):
                dst[size_x + k, t, pl.ds(ROWS + r, ROWS), :] = tile

            rows = strip_readers(size_x, field, k, ylo, yhi)
            corners = strip_readers(size_x, field, size_x, ylo, yhi)
            fill_plane(
                put, lambda y: core[k, pl.ds(y, ROWS), :], *rows, lambda r: side[f, pl.ds(r, ROWS), :], *corners, k, size_y
            )

    def new_value(c, total, drive):
        c2 = c * c
        square = 1.0 - c2
        driving = total - c * (5.0 + c2) - (COUPLING * square * square) * drive
        return jnp.clip(c + TIME_INCREMENT * driving, -1.0, 1.0)

    def phase_pass(step, kept):
        pa, pb, ua = at_step(phase, step), p0 if step % 2 else p1, at_step(solute, step)
        temperatures = warm_own if step == 0 else warm

        def work(at):
            here, above, below = pl.ds(at, ROWS), pl.ds(at + 1, ROWS), pl.ds(at - 1, ROWS)
            plain = pl.ds(at - ROWS, ROWS)
            for g in range(2):
                for t in every:
                    heat = None
                    temperature = temperatures[g, t, plain, :]
                    for k in range(g * size_x, (g + 1) * size_x):
                        old = pa[k][t, here, :]
                        if step == 0:
                            total = pa[(k + 1) % planes][t, here, :] + pa[(k - 1) % planes][t, here, :]
                            total = total + pa[k][t, above, :] + pa[k][t, below, :]
                            total = total + first_p_up[k][t, here, :] + first_p_down[k][t, here, :]
                        else:
                            total = around[k, t, here, :]
                        new = new_value(old, total, ua[k][t, here, :] + temperature)
                        pb[k, t, here, :] = new
                        heat = new - old if heat is None else heat + (new - old)
                    heats[g, t, plain, :] = heat

        sweep(band, work)
        join_bands(pb, kept, band)

    def temperature_pass(step, last):
        ka, kb = small_own if step == 0 else k0 if step % 2 == 0 else k1, k0 if step % 2 else k1
        scale = FREEZING_WARMTH * 0.5 / FACTOR**3
        conduct = TIME_INCREMENT * THERMAL_SPREAD
        tiles_of = [(g, r, t) for g in range(2) for r in range(0, few, ROWS) for t in every]
        sources = [
            sum(heats[g, t, pl.ds(FACTOR * r + j, ROWS, stride=FACTOR), :] for j in range(FACTOR)) for g, r, t in tiles_of
        ]
        pooled = pool_lanes(jnp.concatenate(sources, 0))
        pooled = {key: pooled[ROWS * i : ROWS * i + ROWS] for i, key in enumerate(tiles_of)}
        for g in range(2):
            for r in range(0, few, ROWS):
                count = min(ROWS, few - r)
                at = pl.ds(ROWS + r, ROWS)
                far, near = pl.ds(ROWS + r + 1, ROWS), pl.ds(ROWS + r - 1, ROWS)
                up, down = along_z([ka[g, t, at, :] for t in every], FACTOR)
                for t in every:
                    mine = ka[g, t, at, :]
                    total = 2.0 * ka[1 - g, t, at, :] + up[t] + down[t] + ka[g, t, far, :] + ka[g, t, near, :]
                    new = mine + conduct * (total - 6.0 * mine) + scale * pooled[g, r, t]
                    kb[g, t, at, :] = new
                    if not last:
                        for j in range(FACTOR):
                            warm[g, t, pl.ds(FACTOR * r + j, count, stride=FACTOR), :] = new[:count]
        if not last:
            join_bands(kb, range(2), few)

    def solute_pass(step, last):
        pa, pb = at_step(phase, step), p0 if step % 2 else p1
        ua, ub = at_step(solute, step), u0 if step % 2 else u1
        u_above, u_below = (first_u_up, first_u_down) if step == 0 else (all_of(u_up), all_of(u_down))

        def cell(u, p, p_old, near):
            total_u, total_p = near[0]
            total_w = total_u * total_p
            for un, pn in near[1:]:
                total_u, total_p, total_w = total_u + un, total_p + pn, total_w + un * pn
            flux = (2.0 - p) * (total_u - 6.0 * u) + u * total_p - total_w
            part = 0.5 * (1.0 - PARTITION)
            numer = (0.25 * TIME_INCREMENT * DIFFUSION / part) * flux + (u + 0.5 / part) * (p - p_old)
            return u + numer / (0.5 * (1.0 + PARTITION) / part - p), total_p

        def work(at):
            here, above, below = pl.ds(at, ROWS), pl.ds(at + 1, ROWS), pl.ds(at - 1, ROWS)
            for t in every:
                for k in range(size_x if last else planes):
                    pick = lambda i, w: (ua[i % planes][t, w, :], pb[i % planes, t, w, :])
                    near = [pick(k + 1, here), pick(k - 1, here), pick(k, above), pick(k, below)]
                    near += [(u_above[k][t, here, :], p_up[k, t, here, :]), (u_below[k][t, here, :], p_down[k, t, here, :])]
                    u, p = pick(k, here)
                    new, total = cell(u, p, pa[k][t, here, :], near)
                    ub[k, t, here, :] = new
                    if not last:
                        around[k, t, here, :] = total

        kept = own if last else everything
        follow = None if last else lambda at: keep_shifts(ub, u_up, u_down, at, everything)
        sweep(band, work, follow, lambda at: keep_shifts(pb, p_up, p_down, at, kept))
        if not last:
            join_bands(ub, everything, band)

    def first_shifts(at):
        keep_shifts(p0, p_up, p_down, at, others)
        keep_shifts(u0, u_up, u_down, at, others)

    sweep(band, first_shifts)
    join_bands(p0, others, band)
    join_bands(u0, others, band)
    for step in range(SUBSTEPS):
        last = step == SUBSTEPS - 1
        phase_pass(step, own if last else everything)
        temperature_pass(step, last)
        solute_pass(step, last)

    def from_bands(tile_of, b):
        at = HALO + SLOT * b
        return turn(jnp.where(lane_index(tile_of(b).shape) >= at, tile_of(b), tile_of(b + 1)), -at)

    for src, out in (((p1, p0)[SUBSTEPS % 2 == 0], po_ref), ((u1, u0)[SUBSTEPS % 2 == 0], uo_ref)):
        for k in own:
            for r in range(0, band, ROWS):
                for b in range(BANDS):
                    y = band * b + r - HALO
                    if 0 <= y < size_y:
                        out[k, pl.ds(y, ROWS), :] = from_bands(lambda t: src[k, t, pl.ds(ROWS + r, ROWS), :], b)
    first = me_ref[0] == 0
    short = pick_matrix(LANES, to_ref.shape[2], False)
    last = (k1, k0)[SUBSTEPS % 2 == 0]
    layers = []
    for g in range(2):
        for b in range(BANDS):
            flat[g, pl.ds(ROWS + few * b - HALO // FACTOR, 2 * ROWS), :] = from_bands(lambda t: last[g, t, pl.ds(ROWS, 2 * ROWS), :], b)
        layers.append(exact_dot(flat[g, pl.ds(ROWS, to_ref.shape[0]), :], short))
    for g in range(2):
        to_ref[:, g, :] = jnp.where(first, layers[g], layers[1 - g])


def shifted(x, axis, step):
    count = lax.axis_size(axis)
    return lax.ppermute(x, axis, [(i, (i + step) % count) for i in range(count)])


def swapped(x):
    return lax.ppermute(x, "gx", [(0, 1), (1, 0)])


def at_once(order_parameter, dissolved_species, broad_undercool):
    size_x, size_y, size_z = order_parameter.shape
    f32 = jnp.float32
    planes = 2 * size_x
    me = lax.axis_index("gx").astype(jnp.int32).reshape(1)
    coarse = jnp.transpose(broad_undercool, (0, 2, 1))
    smem = pl.BlockSpec(memory_space=pltpu.SMEM)
    vmem = pl.BlockSpec(memory_space=pltpu.VMEM)
    shape = jax.ShapeDtypeStruct
    band, tiles = band_shape(size_y)
    small = pltpu.CompilerParams(vmem_limit_bytes=SMALL_VMEM)

    partner_p = swapped(order_parameter)
    partner_u = swapped(dissolved_species)

    strip = shape((planes + 2, HALO, LANES), f32)
    to_low, to_high, fine = pl.pallas_call(
        pack_kernel,
        out_shape=[strip] * 2 + [shape((2, size_y, size_z), f32)],
        in_specs=[smem] + [pl.BlockSpec(memory_space=pltpu.HBM)] * 3,
        out_specs=[vmem] * 3,
        scratch_shapes=[pltpu.VMEM(x.shape, f32) for x in (order_parameter, dissolved_species, coarse)]
        + [pltpu.SemaphoreType.DMA((3,))],
        compiler_params=small,
        name="pack",
    )(me, *(pltpu.with_memory_space_constraint(x, pltpu.HBM) for x in (order_parameter, dissolved_species, coarse)))
    zhi = shifted(to_low, "gz", -1)
    zlo = shifted(to_high, "gz", 1)
    strip = shape((strip_height(size_x), LANES), f32)
    side, side_t, to_low, to_high = pl.pallas_call(
        side_kernel,
        out_shape=[shape((planes, band, LANES), f32), shape((2, band, LANES), f32), strip, strip],
        in_specs=[vmem] * 5,
        out_specs=[vmem] * 4,
        compiler_params=small,
        name="side",
    )(order_parameter, dissolved_species, fine, zlo, zhi)
    side_other = swapped(side)
    yhi = shifted(to_low, "gy", -1)
    ylo = shifted(to_high, "gy", 1)
    yhi_other = swapped(yhi)
    ylo_other = swapped(ylo)

    rows = band + 2 * ROWS
    cells, warm = (planes, tiles, rows, LANES), (2, tiles, rows + ROWS, LANES)
    mine = pl.pallas_call(
        own_kernel,
        out_shape=[shape((size_x, *cells[1:]), f32)] * 6 + [shape(warm, f32)] * 2,
        in_specs=[vmem] * 7,
        out_specs=[vmem] * 8,
        compiler_params=pltpu.CompilerParams(vmem_limit_bytes=2 * SMALL_VMEM),
        name="own",
    )(order_parameter, dissolved_species, fine, side, side_t, ylo, yhi)
    flat = pltpu.VMEM((2, size_y // FACTOR + 3 * ROWS, LANES), f32)
    new_p, new_u, new_t = pl.pallas_call(
        step_kernel,
        out_shape=[shape(order_parameter.shape, f32), shape(dissolved_species.shape, f32), shape(coarse.shape, f32)],
        in_specs=[smem] + [vmem] * 13,
        out_specs=[vmem] * 3,
        scratch_shapes=[pltpu.VMEM(cells, f32)] * 9 + [pltpu.VMEM(warm, f32)] * 4 + [flat],
        compiler_params=pltpu.CompilerParams(vmem_limit_bytes=STEP_VMEM),
        name="steps",
    )(me, partner_p, partner_u, side_other, ylo_other, yhi_other, *mine)
    return new_p, new_u, jnp.transpose(new_t, (0, 2, 1))


def per_device(order_parameter, dissolved_species, broad_undercool):
    size_x, size_y, size_z = order_parameter.shape
    whole_x = lax.axis_size("gx") == 2 and broad_undercool.shape[2] * FACTOR == 2 * size_x
    if whole_x and size_x == FACTOR == BANDS and size_y == size_z == LANES == SLOT * BANDS:
        return at_once(order_parameter, dissolved_species, broad_undercool)
    return stepwise(order_parameter, dissolved_species, broad_undercool)


def solution(mesh):
    return jax.shard_map(
        per_device,
        mesh=mesh,
        in_specs=(P("gx", "gy", "gz"), P("gx", "gy", "gz"), P("gy", "gz", None)),
        out_specs=(P("gx", "gy", "gz"), P("gx", "gy", "gz"), P("gy", "gz", None)),
        check_vma=False,
    )
```

```python
import jax
import jax.numpy as jnp
from jax import lax
from jax.experimental import pallas as pl
from jax.experimental.pallas import tpu as pltpu
from jax.sharding import PartitionSpec as P


FACTOR = 4
SUBSTEPS = 4

TIME_INCREMENT = 0.1
COUPLING = 3.0
PARTITION = 0.3
DIFFUSION = 1.0
THERMAL_SPREAD = 1.2
FREEZING_WARMTH = 2.0

LANES = 128
ROWS = 8
HALO = FACTOR * SUBSTEPS
BANDS = 4
SLOT = 2 * HALO
REACH_P = HALO - FACTOR + 1
REACH_U = HALO - FACTOR
SMALL_VMEM = 4 << 20
STEP_VMEM = 24 << 20


def padded_2(cells, sides, width):
    for axis, dim in sides:
        count = lax.axis_size(axis)
        head = lax.slice_in_dim(cells, 0, width, axis=dim)
        tail = lax.slice_in_dim(cells, cells.shape[dim] - width, cells.shape[dim], axis=dim)
        cells = jnp.concatenate(
            [
                lax.ppermute(tail, axis, [(i, (i + 1) % count) for i in range(count)]),
                cells,
                lax.ppermute(head, axis, [((i + 1) % count, i) for i in range(count)]),
            ],
            axis=dim,
        )
    return cells


def laplace_padded(padded):
    center = padded[1:-1, 1:-1, 1:-1]
    total = padded[2:, 1:-1, 1:-1] + padded[:-2, 1:-1, 1:-1]
    total = total + padded[1:-1, 2:, 1:-1] + padded[1:-1, :-2, 1:-1]
    total = total + padded[1:-1, 1:-1, 2:] + padded[1:-1, 1:-1, :-2]
    return total - 6.0 * center


def flux_padded(values, mobility):
    center_v = values[1:-1, 1:-1, 1:-1]
    center_m = mobility[1:-1, 1:-1, 1:-1]
    total = jnp.zeros_like(center_v)
    pairs = (
        (
            values[2:, 1:-1, 1:-1],
            values[:-2, 1:-1, 1:-1],
            mobility[2:, 1:-1, 1:-1],
            mobility[:-2, 1:-1, 1:-1],
        ),
        (
            values[1:-1, 2:, 1:-1],
            values[1:-1, :-2, 1:-1],
            mobility[1:-1, 2:, 1:-1],
            mobility[1:-1, :-2, 1:-1],
        ),
        (
            values[1:-1, 1:-1, 2:],
            values[1:-1, 1:-1, :-2],
            mobility[1:-1, 1:-1, 2:],
            mobility[1:-1, 1:-1, :-2],
        ),
    )
    for upper_v, lower_v, upper_m, lower_m in pairs:
        total = (
            total
            + 0.5 * (upper_m + center_m) * (upper_v - center_v)
            - 0.5 * (center_m + lower_m) * (center_v - lower_v)
        )
    return total


def phase_update(phase_pad, centre_phase, centre_solute, centre_temp):
    square = 1.0 - centre_phase * centre_phase
    driving = (
        laplace_padded(phase_pad)
        + centre_phase
        - centre_phase * centre_phase * centre_phase
        - COUPLING * square * square * (centre_solute + centre_temp)
    )
    return jnp.clip(centre_phase + TIME_INCREMENT * driving, -1.0, 1.0)


def stepwise(order_parameter, dissolved_species, broad_undercool):
    size_x, size_y, size_z = order_parameter.shape
    coarse_x = size_x // FACTOR
    coarse_y = size_y // FACTOR
    coarse_z = size_z // FACTOR
    start_x = lax.axis_index("gx") * coarse_x
    own_block = lax.dynamic_slice_in_dim(broad_undercool, start_x, coarse_x, 2)
    for _ in range(SUBSTEPS):
        planes = own_block
        local_col = jnp.transpose(planes, (2, 0, 1))
        fine_temp = jnp.repeat(jnp.repeat(jnp.repeat(local_col, FACTOR, 0), FACTOR, 1), FACTOR, 2)
        stacked = jnp.stack([order_parameter, dissolved_species])
        padded = padded_2(stacked, (("gx", 1), ("gy", 2), ("gz", 3)), 1)
        solute_pad = padded[1]
        new_phase = phase_update(padded[0], order_parameter, dissolved_species, fine_temp)
        new_pad = padded_2(new_phase, (("gx", 0), ("gy", 1), ("gz", 2)), 1)
        mobility = 0.5 * (1.0 - new_pad)
        change = new_phase - order_parameter
        numer = (
            TIME_INCREMENT * DIFFUSION * flux_padded(solute_pad, mobility)
            + 0.5 * (1.0 + (1.0 - PARTITION) * dissolved_species) * change
        )
        new_solute = dissolved_species + numer / (
            0.5 * (1.0 + PARTITION - (1.0 - PARTITION) * new_phase)
        )
        blocks = (0.5 * change).reshape(coarse_x, FACTOR, coarse_y, FACTOR, coarse_z, FACTOR)
        freezing_warmth_source = jnp.transpose(jnp.mean(blocks, axis=(1, 3, 5)), (1, 2, 0))
        block_pad = padded_2(own_block, (("gx", 2), ("gy", 0), ("gz", 1)), 1)
        own_block = (
            own_block
            + TIME_INCREMENT * THERMAL_SPREAD * laplace_padded(block_pad)
            + FREEZING_WARMTH * freezing_warmth_source
        )
        order_parameter = new_phase
        dissolved_species = new_solute
    vertical_pile = lax.all_gather(own_block, "gx", axis=2, tiled=True)
    return (order_parameter, dissolved_species, vertical_pile)


def lane_index(shape):
    return lax.broadcasted_iota(jnp.int32, shape, 1)


def turn(tile, shift):
    shift = shift % LANES
    return tile if shift == 0 else pltpu.roll(tile, shift, 1)


def choose(pairs, shape, width):
    group = lane_index(shape) // width
    out = pairs[0][1]
    for index, tile in pairs[1:]:
        out = jnp.where(group == index, tile, out)
    return out


def spread_matrix(rows, cols, by_row):
    i = lax.broadcasted_iota(jnp.int32, (rows, cols), 0)
    j = lax.broadcasted_iota(jnp.int32, (rows, cols), 1)
    same = (i // FACTOR == j) if by_row else (i == j // FACTOR)
    return same.astype(jnp.float32)


def pick_matrix(rows, cols, by_row):
    i = lax.broadcasted_iota(jnp.int32, (rows, cols), 0)
    j = lax.broadcasted_iota(jnp.int32, (rows, cols), 1)
    same = (j == i * FACTOR) if by_row else (i == j * FACTOR)
    return same.astype(jnp.float32)


def exact_dot(a, b):
    return jnp.dot(a, b, precision=lax.Precision.HIGHEST, preferred_element_type=jnp.float32)


def pool_lanes(v):
    i = lax.broadcasted_iota(jnp.int32, (LANES, LANES), 0)
    j = lax.broadcasted_iota(jnp.int32, (LANES, LANES), 1)
    same = (i // FACTOR == j // FACTOR).astype(jnp.float32).astype(jnp.bfloat16)
    total = None
    for _ in range(3):
        part = v.astype(jnp.bfloat16)
        v = v - part.astype(jnp.float32)
        term = jnp.dot(part, same, preferred_element_type=jnp.float32)
        total = term if total is None else total + term
    return total


def pack_kernel(me_ref, p_hbm, u_hbm, t_hbm, zlo, zhi, tf_ref, p_ref, u_ref, t_ref, sems):
    size_x, size_y, _ = p_ref.shape
    pairs = ((t_hbm, t_ref), (p_hbm, p_ref), (u_hbm, u_ref))
    copies = [pltpu.make_async_copy(src, dst, sems.at[i]) for i, (src, dst) in enumerate(pairs)]
    for copy in copies:
        copy.start()
    copies[0].wait()
    first = me_ref[0] == 0
    long = spread_matrix(t_ref.shape[2], LANES, False)
    layers = exact_dot(jnp.concatenate([t_ref[:, g, :] for g in range(2)], 0), long)
    count = t_ref.shape[0]
    layers = [layers[count * g : count * g + count] for g in range(2)]
    for g in range(2):
        layer = jnp.where(first, layers[g], layers[1 - g])
        for j in range(FACTOR):
            tf_ref[g, pl.ds(j, count, stride=FACTOR), :] = layer
    shape = (HALO, LANES)
    parts = size_y // HALO

    def strips(ref, at):
        for i in range(ref.shape[0]):
            rows = [ref[i, pl.ds(HALO * g, HALO), :] for g in range(parts)]
            zlo[at + i] = choose([(g, turn(rows[g], HALO * g)) for g in range(parts)], shape, HALO)
            zhi[at + i] = choose([(g, turn(rows[g], HALO * g + HALO)) for g in range(parts)], shape, HALO)

    strips(tf_ref, 2 * size_x)
    copies[1].wait()
    strips(p_ref, 0)
    copies[2].wait()
    strips(u_ref, size_x)


def band_shape(size_y):
    tall = size_y + 2 * HALO
    return tall // BANDS, BANDS * tall // LANES


def side_kernel(p_ref, u_ref, tf_ref, zlo, zhi, side, side_t, ylo, yhi):
    size_x, size_y, _ = p_ref.shape
    band, _ = band_shape(size_y)
    shape = (ROWS, LANES)
    fields = 2 * size_x
    for f in range(fields + 2):
        out = side.at[f] if f < fields else side_t.at[f - fields]
        for r in range(0, band, ROWS):
            pairs = []
            for b in range(BANDS):
                y = band * b + r - HALO
                if 0 <= y < size_y:
                    j, sub = divmod(y, HALO)
                    rows = pl.ds(sub, ROWS)
                    pairs.append((2 * b, turn(zlo[f, rows, :], SLOT * b - HALO * j)))
                    pairs.append((2 * b + 1, turn(zhi[f, rows, :], SLOT * b + HALO - HALO * j)))
            out[pl.ds(r, ROWS), :] = choose(pairs, shape, HALO)
    for out, y, b, below in ((ylo, 0, 0, True), (yhi, size_y, BANDS - 1, False)):
        for field, ref in enumerate((p_ref, u_ref)):
            reach, at = strip_rows(size_x, field, 0)
            first = y if below else y - reach
            r = first + HALO - band * b
            for k in range(size_x):
                out[pl.ds(at + reach * k, reach), :] = ref[k, pl.ds(first, reach), :]
            tiles = [(k, turn(side[field * size_x + k, pl.ds(r, reach), :], SLOT * (k - b))) for k in range(size_x)]
            out[pl.ds(at + reach * size_x, reach), :] = choose(tiles, (reach, LANES), SLOT)
        few = HALO // FACTOR
        _, at = strip_rows(size_x, 2, 0)
        first = y if below else y - HALO
        r = first + HALO - band * b
        for g in range(2):
            out[pl.ds(at + few * g, few), :] = tf_ref[g, pl.ds(first, few, stride=FACTOR), :]
        tiles = [(g, turn(side_t[g, pl.ds(r, few, stride=FACTOR), :], SLOT * (g - b))) for g in range(2)]
        out[pl.ds(at + 2 * few, few), :] = choose(tiles, (few, LANES), SLOT)


def strip_rows(size_x, field, tile):
    reach = (REACH_P, REACH_U, HALO // FACTOR)[field]
    return reach, HALO - REACH_P + (size_x + 1) * sum((REACH_P, REACH_U)[:field]) + reach * tile


def strip_height(size_x):
    rows = strip_rows(size_x, 2, 3)[1]
    return -(-rows // ROWS) * ROWS


def strip_readers(size_x, field, tile, low_ref, high_ref):
    reach, at = strip_rows(size_x, field, tile)

    def low(r):
        return low_ref[pl.ds(at + r - (HALO - reach), ROWS), :]

    def high(r):
        return high_ref[pl.ds(at + r, ROWS), :]

    return low, high


def to_bands(rows_of, halo, tiles):
    lane = lane_index((ROWS, LANES))
    turned = [turn(rows_of(b), HALO + SLOT * b) for b in range(BANDS)]
    out = []
    for t in range(tiles):
        tile = halo
        if t > 0:
            tile = jnp.where(lane < SLOT * t - HALO, turned[t - 1], tile)
        if t < BANDS:
            tile = jnp.where(lane >= SLOT * t + HALO, turned[t], tile)
        out.append(tile)
    return out


def fill_plane(put, core, low, high, side, corner_low, corner_high, slot, size_y):
    band, tiles = band_shape(size_y)
    lane = lane_index((ROWS, LANES))

    for r in range(0, band, ROWS):
        def rows_of(b):
            y = band * b + r - HALO
            return low(r) if y < 0 else high(y - size_y) if y >= size_y else core(y)

        halo = side(r)
        if r < HALO:
            halo = jnp.where(lane < SLOT, turn(corner_low(r), -SLOT * slot), halo)
        if r >= band - HALO:
            halo = jnp.where(lane >= LANES - SLOT, turn(corner_high(r - band + HALO), -SLOT - SLOT * slot), halo)
        for t, tile in enumerate(to_bands(rows_of, halo, tiles)):
            put(t, r, tile)


def along_z(cells, reach):
    lane = lane_index(cells[0].shape)
    tiles = len(cells)
    left = [turn(c, -reach) for c in cells]
    right = [turn(c, reach) for c in cells]
    up = [jnp.where(lane >= LANES - reach, left[t + 1], left[t]) if t + 1 < tiles else left[t] for t in range(tiles)]
    down = [jnp.where(lane < reach, right[t - 1], right[t]) if t > 0 else right[t] for t in range(tiles)]
    return up, down


def keep_shifts(field, up, down, at, some):
    tiles = field.shape[1]
    for k in some:
        above, below = along_z([field[k, t, pl.ds(at, ROWS), :] for t in range(tiles)], 1)
        for t in range(tiles):
            up[k, t, pl.ds(at, ROWS), :] = above[t]
            down[k, t, pl.ds(at, ROWS), :] = below[t]


def join_bands(field, some, rows):
    _, tiles, height, _ = field.shape
    flat = field.reshape(field.shape[0] * tiles * height, LANES)
    lane = lane_index((len(some), LANES))

    def row_of_planes(t, i):
        return pl.ds((some[0] * tiles + t) * height + i, len(some), stride=tiles * height)

    last = [turn(flat[row_of_planes(t, ROWS + rows - 1), :], SLOT) for t in range(tiles)]
    start = [turn(flat[row_of_planes(t, ROWS), :], -SLOT) for t in range(tiles)]
    for t in range(tiles):
        if t > 0:
            tile = last[t - 1] if t == 1 else jnp.where(lane >= SLOT, last[t - 1], last[t - 2])
            flat[row_of_planes(t, ROWS - 1), :] = tile
        if t + 1 < tiles:
            tile = start[t + 1] if t + 2 == tiles else jnp.where(lane < LANES - SLOT, start[t + 1], start[t + 2])
            flat[row_of_planes(t, ROWS + rows), :] = tile


def sweep(rows, work, follow=None, lead=None):
    if lead is not None:
        lead(ROWS)

    def body(i, _):
        at = pl.multiple_of(ROWS + i * ROWS, ROWS)
        if lead is not None:
            lead(at + ROWS)
        if follow is not None:
            follow(at - ROWS)
        work(at)

    lax.fori_loop(0, rows // ROWS, body, None)
    if follow is not None:
        follow(rows)


def own_kernel(p_ref, u_ref, tf_ref, side, side_t, ylo, yhi, p_own, u_own, p_up, p_down, u_up, u_down, warm, small):
    size_x, size_y, _ = p_ref.shape
    band, tiles = band_shape(size_y)
    few = band // FACTOR
    row = lax.broadcasted_iota(jnp.int32, (ROWS, LANES), 0)
    for field, (dst, core) in enumerate(((p_own, p_ref), (u_own, u_ref))):
        for k in range(size_x):
            f = field * size_x + k

            def put(t, r, tile):
                dst[k, t, pl.ds(ROWS + r, ROWS), :] = tile

            rows = strip_readers(size_x, field, k, ylo, yhi)
            corners = strip_readers(size_x, field, size_x, ylo, yhi)
            fill_plane(
                put, lambda y: core[k, pl.ds(y, ROWS), :], *rows, lambda r: side[f, pl.ds(r, ROWS), :], *corners, k, size_y
            )

    def spread(ref, part, r):
        at = strip_rows(size_x, 2, part)[1] + r // FACTOR
        return jnp.where(row < FACTOR, ref[pl.ds(at, 1), :], ref[pl.ds(at + 1, 1), :])

    for g in range(2):
        def put(t, r, tile):
            warm[g, t, pl.ds(r, ROWS), :] = tile

        fill_plane(
            put, lambda y: tf_ref[g, pl.ds(y, ROWS), :],
            lambda r: spread(ylo, g, r), lambda r: spread(yhi, g, r),
            lambda r: side_t[g, pl.ds(r, ROWS), :],
            lambda r: spread(ylo, 2, r), lambda r: spread(yhi, 2, r),
            g, size_y,
        )
        for t in range(tiles):
            small[g, t, pl.ds(ROWS, few), :] = warm[g, t, pl.ds(0, few, stride=FACTOR), :]
    own = range(size_x)

    def shifts(at):
        keep_shifts(p_own, p_up, p_down, at, own)
        keep_shifts(u_own, u_up, u_down, at, own)

    sweep(band, shifts)
    join_bands(p_own, own, band)
    join_bands(u_own, own, band)
    join_bands(small, range(2), few)


def step_kernel(
    me_ref, pp_ref, up_ref, side, ylo, yhi, p_own, u_own, p_up_own, p_down_own, u_up_own, u_down_own, warm_own, small_own,
    po_ref, uo_ref, to_ref,
    p0, p1, u0, u1, around, p_up, p_down, u_up, u_down, warm, heats, k0, k1, flat,
):
    size_x, size_y, _ = pp_ref.shape
    planes = 2 * size_x
    band, tiles = band_shape(size_y)
    shape = (ROWS, LANES)
    lane = lane_index(shape)
    few = band // FACTOR
    every = range(tiles)
    everything, own, others = range(planes), range(size_x), range(size_x, planes)

    def of_planes(mine, ref):
        return [mine.at[k] for k in own] + [ref.at[k] for k in others]

    def all_of(ref):
        return [ref.at[k] for k in everything]

    phase = [of_planes(p_own, p0), all_of(p1), all_of(p0)]
    solute = [of_planes(u_own, u0), all_of(u1), all_of(u0)]
    first_p_up, first_p_down = of_planes(p_up_own, p_up), of_planes(p_down_own, p_down)
    first_u_up, first_u_down = of_planes(u_up_own, u_up), of_planes(u_down_own, u_down)

    def at_step(states, step):
        return states[0] if step == 0 else states[2 - step % 2]

    for field, (dst, core) in enumerate(((p0, pp_ref), (u0, up_ref))):
        for k in range(size_x):
            f = field * size_x + k

            def put(t, r, tile):
                dst[size_x + k, t, pl.ds(ROWS + r, ROWS), :] = tile

            rows = strip_readers(size_x, field, k, ylo, yhi)
            corners = strip_readers(size_x, field, size_x, ylo, yhi)
            fill_plane(
                put, lambda y: core[k, pl.ds(y, ROWS), :], *rows, lambda r: side[f, pl.ds(r, ROWS), :], *corners, k, size_y
            )

    def new_value(c, total, drive):
        c2 = c * c
        square = 1.0 - c2
        driving = total - c * (5.0 + c2) - (COUPLING * square * square) * drive
        return jnp.clip(c + TIME_INCREMENT * driving, -1.0, 1.0)

    def phase_pass(step, kept):
        pa, pb, ua = at_step(phase, step), p0 if step % 2 else p1, at_step(solute, step)
        temperatures = warm_own if step == 0 else warm

        for r in range(0, band, ROWS):
            at = ROWS + r
            here, above, below, plain = pl.ds(at, ROWS), pl.ds(at + 1, ROWS), pl.ds(at - 1, ROWS), pl.ds(r, ROWS)
            for g in range(2):
                heat = [None] * tiles
                temperature = [temperatures[g, t, plain, :] for t in every]
                for k in range(g * size_x, (g + 1) * size_x):
                    fresh = []
                    for t in every:
                        old = pa[k][t, here, :]
                        if step == 0:
                            total = pa[(k + 1) % planes][t, here, :] + pa[(k - 1) % planes][t, here, :]
                            total = total + pa[k][t, above, :] + pa[k][t, below, :]
                            total = total + first_p_up[k][t, here, :] + first_p_down[k][t, here, :]
                        else:
                            total = around[k, t, here, :]
                        new = new_value(old, total, ua[k][t, here, :] + temperature[t])
                        pb[k, t, here, :] = new
                        heat[t] = new - old if heat[t] is None else heat[t] + (new - old)
                        fresh.append(new)
                    if k in kept:
                        up, down = along_z(fresh, 1)
                        for t in every:
                            p_up[k, t, here, :] = up[t]
                            p_down[k, t, here, :] = down[t]
                for t in every:
                    heats[g, t, plain, :] = heat[t]
        join_bands(pb, kept, band)

    def temperature_pass(step, last):
        ka, kb = small_own if step == 0 else k0 if step % 2 == 0 else k1, k0 if step % 2 else k1
        scale = FREEZING_WARMTH * 0.5 / FACTOR**3
        conduct = TIME_INCREMENT * THERMAL_SPREAD
        tiles_of = [(g, r, t) for g in range(2) for r in range(0, few, ROWS) for t in every]
        sources = [
            sum(heats[g, t, pl.ds(FACTOR * r + j, ROWS, stride=FACTOR), :] for j in range(FACTOR)) for g, r, t in tiles_of
        ]
        pooled = pool_lanes(jnp.concatenate(sources, 0))
        pooled = {key: pooled[ROWS * i : ROWS * i + ROWS] for i, key in enumerate(tiles_of)}
        for g in range(2):
            for r in range(0, few, ROWS):
                count = min(ROWS, few - r)
                at = pl.ds(ROWS + r, ROWS)
                far, near = pl.ds(ROWS + r + 1, ROWS), pl.ds(ROWS + r - 1, ROWS)
                up, down = along_z([ka[g, t, at, :] for t in every], FACTOR)
                for t in every:
                    mine = ka[g, t, at, :]
                    total = 2.0 * ka[1 - g, t, at, :] + up[t] + down[t] + ka[g, t, far, :] + ka[g, t, near, :]
                    new = mine + conduct * (total - 6.0 * mine) + scale * pooled[g, r, t]
                    kb[g, t, at, :] = new
                    if not last:
                        for j in range(FACTOR):
                            warm[g, t, pl.ds(FACTOR * r + j, count, stride=FACTOR), :] = new[:count]
        if not last:
            join_bands(kb, range(2), few)

    def solute_pass(step, last):
        pa, pb = at_step(phase, step), p0 if step % 2 else p1
        ua, ub = at_step(solute, step), u0 if step % 2 else u1
        u_above, u_below = (first_u_up, first_u_down) if step == 0 else (all_of(u_up), all_of(u_down))

        def cell(u, p, p_old, near):
            total_u, total_p = near[0]
            total_w = total_u * total_p
            for un, pn in near[1:]:
                total_u, total_p, total_w = total_u + un, total_p + pn, total_w + un * pn
            flux = (2.0 - p) * (total_u - 6.0 * u) + u * total_p - total_w
            part = 0.5 * (1.0 - PARTITION)
            numer = (0.25 * TIME_INCREMENT * DIFFUSION / part) * flux + (u + 0.5 / part) * (p - p_old)
            return u + numer / (0.5 * (1.0 + PARTITION) / part - p), total_p

        def work(at):
            here, above, below = pl.ds(at, ROWS), pl.ds(at + 1, ROWS), pl.ds(at - 1, ROWS)
            for t in every:
                for k in range(size_x if last else planes):
                    pick = lambda i, w: (ua[i % planes][t, w, :], pb[i % planes, t, w, :])
                    near = [pick(k + 1, here), pick(k - 1, here), pick(k, above), pick(k, below)]
                    near += [(u_above[k][t, here, :], p_up[k, t, here, :]), (u_below[k][t, here, :], p_down[k, t, here, :])]
                    u, p = pick(k, here)
                    new, total = cell(u, p, pa[k][t, here, :], near)
                    ub[k, t, here, :] = new
                    if not last:
                        around[k, t, here, :] = total

        follow = None if last else lambda at: keep_shifts(ub, u_up, u_down, at, everything)
        if last:
            for r in range(0, band, ROWS):
                work(ROWS + r)
        else:
            sweep(band, work, follow)
        if not last:
            join_bands(ub, everything, band)

    def first_shifts(at):
        keep_shifts(p0, p_up, p_down, at, others)
        keep_shifts(u0, u_up, u_down, at, others)

    sweep(band, first_shifts)
    join_bands(p0, others, band)
    join_bands(u0, others, band)
    for step in range(SUBSTEPS):
        last = step == SUBSTEPS - 1
        phase_pass(step, own if last else everything)
        temperature_pass(step, last)
        solute_pass(step, last)

    def from_bands(tile_of, b):
        at = HALO + SLOT * b
        return turn(jnp.where(lane_index(tile_of(b).shape) >= at, tile_of(b), tile_of(b + 1)), -at)

    for src, out in (((p1, p0)[SUBSTEPS % 2 == 0], po_ref), ((u1, u0)[SUBSTEPS % 2 == 0], uo_ref)):
        for k in own:
            for r in range(0, band, ROWS):
                for b in range(BANDS):
                    y = band * b + r - HALO
                    if 0 <= y < size_y:
                        out[k, pl.ds(y, ROWS), :] = from_bands(lambda t: src[k, t, pl.ds(ROWS + r, ROWS), :], b)
    first = me_ref[0] == 0
    short = pick_matrix(LANES, to_ref.shape[2], False)
    last = (k1, k0)[SUBSTEPS % 2 == 0]
    layers = []
    for g in range(2):
        for b in range(BANDS):
            flat[g, pl.ds(ROWS + few * b - HALO // FACTOR, 2 * ROWS), :] = from_bands(lambda t: last[g, t, pl.ds(ROWS, 2 * ROWS), :], b)
        layers.append(exact_dot(flat[g, pl.ds(ROWS, to_ref.shape[0]), :], short))
    for g in range(2):
        to_ref[:, g, :] = jnp.where(first, layers[g], layers[1 - g])


def shifted(x, axis, step):
    count = lax.axis_size(axis)
    return lax.ppermute(x, axis, [(i, (i + step) % count) for i in range(count)])


def swapped(x):
    return lax.ppermute(x, "gx", [(0, 1), (1, 0)])


def at_once(order_parameter, dissolved_species, broad_undercool):
    size_x, size_y, size_z = order_parameter.shape
    f32 = jnp.float32
    planes = 2 * size_x
    me = lax.axis_index("gx").astype(jnp.int32).reshape(1)
    coarse = jnp.transpose(broad_undercool, (0, 2, 1))
    smem = pl.BlockSpec(memory_space=pltpu.SMEM)
    vmem = pl.BlockSpec(memory_space=pltpu.VMEM)
    shape = jax.ShapeDtypeStruct
    band, tiles = band_shape(size_y)
    small = pltpu.CompilerParams(vmem_limit_bytes=SMALL_VMEM)

    partner_p = swapped(order_parameter)
    partner_u = swapped(dissolved_species)

    strip = shape((planes + 2, HALO, LANES), f32)
    to_low, to_high, fine = pl.pallas_call(
        pack_kernel,
        out_shape=[strip] * 2 + [shape((2, size_y, size_z), f32)],
        in_specs=[smem] + [pl.BlockSpec(memory_space=pltpu.HBM)] * 3,
        out_specs=[vmem] * 3,
        scratch_shapes=[pltpu.VMEM(x.shape, f32) for x in (order_parameter, dissolved_species, coarse)]
        + [pltpu.SemaphoreType.DMA((3,))],
        compiler_params=small,
        name="pack",
    )(me, *(pltpu.with_memory_space_constraint(x, pltpu.HBM) for x in (order_parameter, dissolved_species, coarse)))
    zhi = shifted(to_low, "gz", -1)
    zlo = shifted(to_high, "gz", 1)
    strip = shape((strip_height(size_x), LANES), f32)
    side, side_t, to_low, to_high = pl.pallas_call(
        side_kernel,
        out_shape=[shape((planes, band, LANES), f32), shape((2, band, LANES), f32), strip, strip],
        in_specs=[vmem] * 5,
        out_specs=[vmem] * 4,
        compiler_params=small,
        name="side",
    )(order_parameter, dissolved_species, fine, zlo, zhi)
    side_other = swapped(side)
    yhi = shifted(to_low, "gy", -1)
    ylo = shifted(to_high, "gy", 1)
    yhi_other = swapped(yhi)
    ylo_other = swapped(ylo)

    rows = band + 2 * ROWS
    cells, warm = (planes, tiles, rows, LANES), (2, tiles, rows + ROWS, LANES)
    mine = pl.pallas_call(
        own_kernel,
        out_shape=[shape((size_x, *cells[1:]), f32)] * 6 + [shape(warm, f32)] * 2,
        in_specs=[vmem] * 7,
        out_specs=[vmem] * 8,
        compiler_params=pltpu.CompilerParams(vmem_limit_bytes=2 * SMALL_VMEM),
        name="own",
    )(order_parameter, dissolved_species, fine, side, side_t, ylo, yhi)
    flat = pltpu.VMEM((2, size_y // FACTOR + 3 * ROWS, LANES), f32)
    new_p, new_u, new_t = pl.pallas_call(
        step_kernel,
        out_shape=[shape(order_parameter.shape, f32), shape(dissolved_species.shape, f32), shape(coarse.shape, f32)],
        in_specs=[smem] + [vmem] * 13,
        out_specs=[vmem] * 3,
        scratch_shapes=[pltpu.VMEM(cells, f32)] * 9 + [pltpu.VMEM(warm, f32)] * 4 + [flat],
        compiler_params=pltpu.CompilerParams(vmem_limit_bytes=STEP_VMEM),
        name="steps",
    )(me, partner_p, partner_u, side_other, ylo_other, yhi_other, *mine)
    return new_p, new_u, jnp.transpose(new_t, (0, 2, 1))


def per_device(order_parameter, dissolved_species, broad_undercool):
    size_x, size_y, size_z = order_parameter.shape
    whole_x = lax.axis_size("gx") == 2 and broad_undercool.shape[2] * FACTOR == 2 * size_x
    if whole_x and size_x == FACTOR == BANDS and size_y == size_z == LANES == SLOT * BANDS:
        return at_once(order_parameter, dissolved_species, broad_undercool)
    return stepwise(order_parameter, dissolved_species, broad_undercool)


def solution(mesh):
    return jax.shard_map(
        per_device,
        mesh=mesh,
        in_specs=(P("gx", "gy", "gz"), P("gx", "gy", "gz"), P("gy", "gz", None)),
        out_specs=(P("gx", "gy", "gz"), P("gx", "gy", "gz"), P("gy", "gz", None)),
        check_vma=False,
    )
```
